256 devices in a mesh: vocab: 64 (over y, z, core), hidden: 4 (over x).
Axes of the slice: x: 4, y: 4, z: 8, core: 2. Of those that a mesh axis runs over, the one named last changes fastest.
Arguments:
- states: bfloat16 [1024, 7168], P(('vocab', 'hidden')), may hold values from -32 to 32
- head: bfloat16 [7168, 129280], P('hidden', 'vocab'), may hold values from -1 to 1
Outputs:
- logp: float32 [1024, 129280], P('hidden', 'vocab')
The draws below stay inside these ranges and needn't reach their ends.
All inputs are finite; a program needn't handle non-finite values.
Results may differ from the reference program's by a relative error of at most 0.0003.
Values may be sent and summed in bfloat16 or wider, within the bound.
A program may use at most 128 MiB of HBM per device.

```python
import math
import jax
import jax.numpy as jnp

D = 7168
V = 129280
ROWS = 1024


def head_column(key, column):
    column_key = jax.random.fold_in(jax.random.fold_in(key, 7), column)
    return jax.random.normal(column_key, (D,), jnp.float32) * D ** (-0.5)


def draw_head(key, part):
    columns = jax.vmap(lambda column: head_column(key, column))(jnp.arange(V, dtype=jnp.int32))
    return jnp.clip(columns.T, -1.0, 1.0).astype(jnp.bfloat16)


def draw_states(key, part):
    base_key = jax.random.fold_in(key, 11)
    keys = jax.random.split(base_key, 1)
    return jnp.clip(jax.random.normal(keys[0], (ROWS, D), jnp.float32), -6.0, 6.0).astype(jnp.bfloat16)


def setup_inputs(seed: int = 0) -> dict:
    key_list = jax.random.split(jax.random.key(seed), 3)
    states = draw_states(jax.random.fold_in(key_list[2], 71), 0)
    head = draw_head(jax.random.fold_in(key_list[2], 71), 0)
    return {"states": states, "head": head}


sharpness = 4.0
minp_offset = math.log(10.0)
logp_floor = 30.0


def reference(states, head):
    logits = jnp.dot(states, head, preferred_element_type=jnp.float32)
    top = jnp.max(logits, axis=1, keepdims=True)
    shifted = logits - top
    gated = shifted + jax.nn.log_sigmoid(sharpness * (shifted + minp_offset))
    total = jnp.sum(jnp.exp(gated), axis=1, keepdims=True)
    return jnp.maximum(gated - jnp.log(total), -logp_floor)
```

```python
import functools
import math

import jax
import jax.numpy as jnp
from jax import lax
from jax.experimental import pallas as pl
from jax.experimental.pallas import tpu as pltpu
from jax.sharding import Mesh
from jax.sharding import PartitionSpec as P

MESH = pl.DeviceIdType.MESH
VOCAB = ("y", "z", "c")
VOCAB_HIDDEN = ("y", "z", "c", "x")
NX, NY, NZ, NC = 4, 4, 8, 2

sharpness = 4.0
minp_offset = math.log(10.0)
logp_floor = 30.0

BLOCK = 128
HALF = 64
PIECE = 16
LOCAL = 4
DEPTH = 1792
COLS = 2020
CHUNKS = ((0, 512), (512, 512), (1024, 512), (1536, 484))
POWER = 7


def coded(v):
    v2 = v * v
    v3 = v2 * v
    return (v3 * (v2 * v2)).astype(jnp.bfloat16)


def decoded(w):
    w = w.astype(jnp.float32)
    r = jnp.exp2(jnp.log2(jnp.abs(w)) * (1.0 / POWER))
    return jnp.where(w < 0.0, -r, r)


def kernel(
    states, head, gated_out, lnt_out,
    weights, xin, st, prod, s1out, s1in, s2out, s2in, acc, col, ex1, ex2,
    w_sem, xl_sem, xs_sem, xr_sem, ys_sem, yr_sem, zs_sem, zr_sem, cs_sem, cr_sem,
    s1s_sem, s1r_sem, s2s_sem, s2r_sem, e1s_sem, e1r_sem, e2s_sem, e2r_sem, o_sem,
):
    x, y, z, c = (lax.axis_index(n) for n in ("x", "y", "z", "c"))
    q = y * NC + c

    def at(axis, index):
        here = {"x": x, "y": y, "z": z, "c": c}
        here[axis] = index
        return (here["y"], here["z"], here["c"], here["x"])

    def in_plane(index):
        return (index // NC, z, index % NC, x)

    def remote(src, dst, send, recv, device):
        return pltpu.make_async_remote_copy(
            src_ref=src, dst_ref=dst, send_sem=send, recv_sem=recv,
            device_id=device, device_id_type=MESH,
        )

    w_copies = [
        pltpu.make_async_copy(
            head.at[pl.ds(256 * k, 256), :], weights.at[pl.ds(256 * k, 256), :], w_sem.at[k]
        )
        for k in range(7)
    ]
    for copy in w_copies:
        copy.start()
    own_piece = pltpu.make_async_copy(
        states.at[:, pl.ds(pl.multiple_of(x * DEPTH, 128), DEPTH)], xin.at[x], xl_sem
    )
    own_piece.start()

    barrier = pltpu.get_barrier_semaphore()
    partners = [at("x", (x + k) % NX) for k in range(1, NX)]
    partners += [in_plane((q + k) % (NY * NC)) for k in range(1, NY * NC)]
    partners += [at("z", (z + k) % NZ) for k in range(1, NZ)]
    for device in partners:
        pl.semaphore_signal(barrier, inc=1, device_id=device, device_id_type=MESH)
    pl.semaphore_wait(barrier, len(partners))

    x_copies = []
    for k in range(1, NX):
        to = (x + k) % NX
        x_copies.append(remote(
            states.at[:, pl.ds(pl.multiple_of(to * DEPTH, 128), DEPTH)], xin.at[x],
            xs_sem.at[k - 1], xr_sem.at[k - 1], at("x", to),
        ))
        x_copies[-1].start()
    own_piece.wait()
    for copy in x_copies:
        copy.wait_recv()
    mine = pl.multiple_of(c * HALF + y * PIECE, PIECE)
    pieces = [xin[k].astype(jnp.float32) for k in range(NX)]
    st[z, pl.ds(mine, PIECE), :] = jnp.concatenate(pieces, axis=0).astype(jnp.bfloat16)

    y_copies = []
    for k in range(1, NY):
        here = st.at[z, pl.ds(mine, PIECE), :]
        y_copies.append(remote(
            here, here, ys_sem.at[k - 1], yr_sem.at[k - 1], at("y", (y + k) % NY)
        ))
        y_copies[-1].start()
    for copy in y_copies:
        copy.wait_recv()

    half = pl.multiple_of(c * HALF, HALF)

    def along_z(direction, step, block, rows, count):
        there = st.at[block, pl.ds(rows, count), :]
        to = (z + 1) % NZ if direction == 0 else (z + NZ - 1) % NZ
        return remote(
            there, there, zs_sem.at[direction, step], zr_sem.at[direction, step], at("z", to)
        )

    def to_sibling(b, block):
        there = st.at[block, pl.ds(half, HALF), :]
        return remote(there, there, cs_sem.at[b], cr_sem.at[b], at("c", 1 - c))

    along_z(0, 1, z, half, HALF).start()
    along_z(1, 1, z, half, HALF).start()
    to_sibling(0, z).start()
    for copy in w_copies:
        copy.wait()

    right, left, across = (x + 1) % NX, (x + NX - 1) % NX, (x + 2) % NX

    def first_hop(b, h):
        return remote(
            s1out.at[b, h], s1in.at[b, h], s1s_sem.at[b, h], s1r_sem.at[b, h],
            at("x", right if h == 0 else left),
        )

    def second_hop(b, h):
        return remote(
            s2out.at[b, h], s2in.at[b, h], s2s_sem.at[b, h], s2r_sem.at[b, h],
            at("x", right if h == 0 else left),
        )

    def rows_for(h, d):
        return pl.ds(pl.multiple_of(h * HALF + d * PIECE, PIECE), PIECE)

    def block_at(b):
        s = (b + 1) // 2
        return (z + s * (1 - 2 * (b % 2)) + NZ) % NZ

    def step(b, carry):
        for s in (1, 2, 3):
            @pl.when(b == 2 * s - 1)
            def _():
                behind, ahead = (z + NZ - s) % NZ, (z + s) % NZ
                for direction, block in ((0, behind), (1, ahead)):
                    along_z(direction, s, block, half, HALF).wait_recv()
                    if s < 3:
                        along_z(direction, s + 1, block, half, HALF).start()
                    else:
                        rows = pl.multiple_of(half + 32 * direction, 32)
                        along_z(direction, 4, block, rows, 32).start()
                    to_sibling(b + direction, block).start()

        @pl.when(b == 7)
        def _():
            block = (z + 4) % NZ
            for direction in (0, 1):
                rows = pl.multiple_of(half + 32 * direction, 32)
                along_z(direction, 4, block, rows, 32).wait_recv()
            to_sibling(7, block).start()

        @pl.when(b < NZ)
        def _():
            block = block_at(b)
            to_sibling(b, block).wait_recv()
            for lo, n in CHUNKS:
                prod[b, :, lo:lo + n] = jnp.dot(
                    st[block], weights[:, lo:lo + n], preferred_element_type=jnp.float32
                )
            for h in (0, 1):
                for lo, n in CHUNKS:
                    s1out[b, h, :, lo:lo + n] = coded(prod[b, rows_for(h, across), lo:lo + n])
                first_hop(b, h).start()

        @pl.when(jnp.logical_and(b >= 1, b < NZ + 1))
        def _():
            p = b - 1
            for h in (0, 1):
                to = right if h == 0 else left
                for lo, n in CHUNKS:
                    s2out[p, h, 16 * (1 - h):16 * (1 - h) + 16, lo:lo + n] = coded(
                        prod[p, rows_for(1 - h, to), lo:lo + n]
                    )
            for h in (0, 1):
                to = right if h == 0 else left
                first_hop(p, h).wait_recv()
                for lo, n in CHUNKS:
                    s2out[p, h, 16 * h:16 * h + 16, lo:lo + n] = coded(
                        prod[p, rows_for(h, to), lo:lo + n] + decoded(s1in[p, h, :, lo:lo + n])
                    )
                second_hop(p, h).start()

        @pl.when(b >= 2)
        def _():
            p = b - 2
            block = block_at(p)
            second_hop(p, 0).wait_recv()
            second_hop(p, 1).wait_recv()
            for h in (0, 1):
                top = jnp.full((PIECE, 1), -jnp.inf, jnp.float32)
                for lo, n in CHUNKS:
                    logits = prod[p, rows_for(h, x), lo:lo + n] + (
                        decoded(s2in[p, 0, 16 * h:16 * h + 16, lo:lo + n])
                        + decoded(s2in[p, 1, 16 * h:16 * h + 16, lo:lo + n])
                    )
                    acc[block, 16 * h:16 * h + 16, lo:lo + n] = logits
                    top = jnp.maximum(top, jnp.max(logits, axis=1, keepdims=True))
                col[block, 16 * h:16 * h + 16, :] = jnp.broadcast_to(top, (PIECE, 128))

        return carry

    lax.fori_loop(0, NZ + 2, step, 0)

    def exchanged(combine, base):
        row = jnp.transpose(col[...].reshape(256, 128))[0:1, :]
        ex1[base + q] = row
        first = [
            remote(
                ex1.at[base + q], ex1.at[base + q], e1s_sem.at[base + k], e1r_sem.at[base + k],
                in_plane((q + k) % (NY * NC)),
            )
            for k in range(1, NY * NC)
        ]
        for copy in first:
            copy.start()
        for copy in first:
            copy.wait_recv()
        row = ex1[base]
        for k in range(1, NY * NC):
            row = combine(row, ex1[base + k])
        ex2[base + z] = row
        second = [
            remote(
                ex2.at[base + z], ex2.at[base + z], e2s_sem.at[base + k], e2r_sem.at[base + k],
                at("z", (z + k) % NZ),
            )
            for k in range(1, NZ)
        ]
        for copy in second:
            copy.start()
        for copy in second:
            copy.wait_recv()
        row = ex2[base]
        for k in range(1, NZ):
            row = combine(row, ex2[base + k])
        return jnp.transpose(jnp.broadcast_to(row, (128, 256))), first + second

    top, sent_top = exchanged(jnp.maximum, 0)
    col[...] = top.reshape(NZ, 32, 128)

    def filter_rows(block, carry):
        for h in (0, 1):
            t = col[block, 16 * h:16 * h + 16, 0:1]
            total = jnp.zeros((PIECE, 1), jnp.float32)
            for lo, n in CHUNKS:
                shifted = acc[block, 16 * h:16 * h + 16, lo:lo + n] - t
                u = sharpness * (shifted + minp_offset)
                gated = shifted + (jnp.minimum(u, 0.0) - jnp.log1p(jnp.exp(-jnp.abs(u))))
                acc[block, 16 * h:16 * h + 16, lo:lo + n] = gated
                total = total + jnp.sum(jnp.exp(gated), axis=1, keepdims=True)
            col[block, 16 * h:16 * h + 16, :] = jnp.broadcast_to(total, (PIECE, 128))
        pltpu.make_async_copy(acc.at[block], gated_out.at[block], o_sem.at[block]).start()
        return carry

    lax.fori_loop(0, NZ, filter_rows, 0)
    total, sent_total = exchanged(jnp.add, 8)
    lnt_out[...] = jnp.log(total)

    for copy in x_copies + y_copies + sent_top + sent_total:
        copy.wait_send()
    for direction in (0, 1):
        for s in (1, 2, 3):
            along_z(direction, s, z, half, HALF).wait_send()
        along_z(direction, 4, z, half, 32).wait_send()

    def settle(b, carry):
        to_sibling(b, z).wait_send()
        for h in (0, 1):
            first_hop(b, h).wait_send()
            second_hop(b, h).wait_send()
        pltpu.make_async_copy(acc.at[b], gated_out.at[b], o_sem.at[b]).wait()
        return carry

    lax.fori_loop(0, NZ, settle, 0)


def body(states, head):
    dma = pltpu.SemaphoreType.DMA
    f32, bf16 = jnp.float32, jnp.bfloat16
    gated, lnt = pl.pallas_call(
        kernel,
        out_shape=(
            jax.ShapeDtypeStruct((NZ, 32, COLS), f32),
            jax.ShapeDtypeStruct((256, 128), f32),
        ),
        in_specs=[pl.BlockSpec(memory_space=pl.ANY)] * 2,
        out_specs=(
            pl.BlockSpec(memory_space=pl.ANY),
            pl.BlockSpec(memory_space=pltpu.VMEM),
        ),
        scratch_shapes=[
            pltpu.VMEM((DEPTH, COLS), bf16),
            pltpu.VMEM((NX, LOCAL, DEPTH), bf16),
            pltpu.VMEM((NZ, BLOCK, DEPTH), bf16),
            pltpu.VMEM((NZ, BLOCK, COLS), f32),
            pltpu.VMEM((NZ, 2, PIECE, COLS), bf16),
            pltpu.VMEM((NZ, 2, PIECE, COLS), bf16),
            pltpu.VMEM((NZ, 2, 2 * PIECE, COLS), bf16),
            pltpu.VMEM((NZ, 2, 2 * PIECE, COLS), bf16),
            pltpu.VMEM((NZ, 32, COLS), f32),
            pltpu.VMEM((NZ, 32, 128), f32),
            pltpu.VMEM((16, 1, 256), f32),
            pltpu.VMEM((16, 1, 256), f32),
            dma((7,)),
            dma,
            dma((3,)), dma((3,)),
            dma((3,)), dma((3,)),
            dma((2, 5)), dma((2, 5)),
            dma((8,)), dma((8,)),
            dma((8, 2)), dma((8, 2)),
            dma((8, 2)), dma((8, 2)),
            dma((16,)), dma((16,)),
            dma((16,)), dma((16,)),
            dma((8,)),
        ],
        compiler_params=pltpu.CompilerParams(
            collective_id=0, has_side_effects=True, vmem_limit_bytes=60 * 1024 * 1024
        ),
        name="minp",
    )(states, head)
    return jnp.maximum(gated.reshape(256, COLS) - lnt[:, :1], -logp_floor)


def solution(mesh):
    torus = Mesh(
        mesh.devices.reshape(NY, NZ, NC, NX),
        ("y", "z", "c", "x"),
    )
    return jax.shard_map(
        body,
        mesh=torus,
        in_specs=(P(VOCAB_HIDDEN, None), P("x", VOCAB)),
        out_specs=P("x", VOCAB),
        check_vma=False,
    )
```

```python
import math

import jax
import jax.numpy as jnp
from jax import lax
from jax.experimental import pallas as pl
from jax.experimental.pallas import tpu as pltpu
from jax.sharding import Mesh
from jax.sharding import PartitionSpec as P

MESH = pl.DeviceIdType.MESH
VOCAB = ("y", "z", "c")
VOCAB_HIDDEN = ("y", "z", "c", "x")
NX, NY, NZ, NC = 4, 4, 8, 2

sharpness = 4.0
minp_offset = math.log(10.0)
logp_floor = 30.0

BLOCK = 128
HALF = 64
PIECE = 16
LOCAL = 4
OWNED = 256
DEPTH = 1792
COLS = 2020
CHUNKS = ((0, 512), (512, 512), (1024, 512), (1536, 484))
POWER = 7
STEP = 224
TAIL = 9 * STEP

PLANE = [(dy, dx) for dy in range(NY) for dx in range(NX) if dy or dx]
PLANE.sort(key=lambda p: -(min(p[0], NY - p[0]) + min(p[1], NX - p[1])))
FAR = [(dy, dz) for dy in range(NY) for dz in range(NZ) if dy or dz]
FAR.sort(key=lambda p: -(min(p[0], NY - p[0]) + min(p[1], NZ - p[1])))


def coded(v):
    v2 = v * v
    v3 = v2 * v
    return (v3 * (v2 * v2)).astype(jnp.bfloat16)


def decoded(w):
    w = w.astype(jnp.float32)
    r = jnp.exp2(jnp.log2(jnp.abs(w)) * (1.0 / POWER))
    return jnp.where(w < 0.0, -r, r)


def lane_max(v):
    n = v.shape[1]
    best = v[:, 0:128]
    for lo in range(128, n, 128):
        part = v[:, lo:min(lo + 128, n)]
        if part.shape[1] < 128:
            fill = jnp.full((v.shape[0], 128 - part.shape[1]), -jnp.inf, v.dtype)
            part = jnp.concatenate([part, fill], axis=1)
        best = jnp.maximum(best, part)
    return best


def kernel(
    states, head, gated_out, lnt_out,
    raw, weights, xin, st, prod, s1out, s1in, s2out, s2in, acc, logits_t, gated, col, exc, exn,
    w_sem, xl_sem, xs_sem, xr_sem, zs_sem, zr_sem, cs_sem, cr_sem,
    s1s_sem, s1r_sem, s2s_sem, s2r_sem, ecs_sem, ecr_sem, ens_sem, enr_sem, o_sem,
):
    x, y, z, c = (lax.axis_index(n) for n in ("x", "y", "z", "c"))

    def at(dy=0, dz=0, dx=0, dc=0):
        return (
            (y + dy) % NY if dy else y,
            (z + dz) % NZ if dz else z,
            1 - c if dc else c,
            (x + dx) % NX if dx else x,
        )

    def remote(src, dst, send, recv, device):
        return pltpu.make_async_remote_copy(
            src_ref=src, dst_ref=dst, send_sem=send, recv_sem=recv,
            device_id=device, device_id_type=MESH,
        )

    w_copy = pltpu.make_async_copy(head, raw, w_sem)
    w_copy.start()
    own_piece = pltpu.make_async_copy(
        states.at[:, pl.ds(pl.multiple_of(x * DEPTH, 128), DEPTH)], xin.at[y * NX + x], xl_sem
    )
    own_piece.start()

    barrier = pltpu.get_barrier_semaphore()
    partners = [at(dy=dy, dx=dx) for dy, dx in PLANE]
    partners += [at(dz=1), at(dz=NZ - 1), at(dc=1)]
    for device in partners:
        pl.semaphore_signal(barrier, inc=1, device_id=device, device_id_type=MESH)
    pl.semaphore_wait(barrier, len(partners))

    x_copies = []
    for k, (dy, dx) in enumerate(PLANE):
        to = (x + dx) % NX
        x_copies.append(remote(
            states.at[:, pl.ds(pl.multiple_of(to * DEPTH, 128), DEPTH)], xin.at[y * NX + x],
            xs_sem.at[k], xr_sem.at[k], at(dy=dy, dx=dx),
        ))
        x_copies[-1].start()

    w_copy.wait()
    for lo in range(0, COLS, 256):
        n = min(256, COLS - lo)
        weights[:, lo:lo + n] = jnp.transpose(raw[lo:lo + n, :])

    own_piece.wait()
    for copy in x_copies:
        copy.wait_recv()
    half = pl.multiple_of(c * HALF, HALF)
    for j in range(NY):
        pieces = [xin[j * NX + k].astype(jnp.float32) for k in range(NX)]
        st[0, pl.ds(pl.multiple_of(half + j * PIECE, PIECE), PIECE), :] = jnp.concatenate(
            pieces, axis=0
        ).astype(jnp.bfloat16)

    def along_z(direction, s):
        source = 0 if s == 1 else 2 * s - 3 + direction
        target = 2 * s - 1 + direction if s < 4 else 7
        if s < 4:
            rows = pl.ds(half, HALF)
        else:
            rows = pl.ds(pl.multiple_of(half + 32 * direction, 32), 32)
        return remote(
            st.at[source, rows, :], st.at[target, rows, :],
            zs_sem.at[direction, s], zr_sem.at[direction, s],
            at(dz=1 if direction == 0 else NZ - 1),
        )

    def to_sibling(b):
        there = st.at[b, pl.ds(half, HALF), :]
        return remote(there, there, cs_sem.at[b], cr_sem.at[b], at(dc=1))

    to_sibling(0).start()
    along_z(0, 1).start()
    along_z(1, 1).start()

    right, left, across = (x + 1) % NX, (x + NX - 1) % NX, (x + 2) % NX

    def first_hop(b, h):
        return remote(
            s1out.at[b, h], s1in.at[b, h], s1s_sem.at[b, h], s1r_sem.at[b, h],
            at(dx=1 if h == 0 else NX - 1),
        )

    def second_hop(b, h):
        return remote(
            s2out.at[b, h], s2in.at[b, h], s2s_sem.at[b, h], s2r_sem.at[b, h],
            at(dx=1 if h == 0 else NX - 1),
        )

    def rows_for(h, d):
        return pl.ds(pl.multiple_of(h * HALF + d * PIECE, PIECE), PIECE)

    def multiply(b, carry):
        to_sibling(b).wait_recv()
        for lo, n in CHUNKS:
            prod[b, :, lo:lo + n] = jnp.dot(
                st[b], weights[:, lo:lo + n], preferred_element_type=jnp.float32
            )
        for h in (0, 1):
            for lo, n in CHUNKS:
                s1out[b, h, :, lo:lo + n] = coded(prod[b, rows_for(h, across), lo:lo + n])
            first_hop(b, h).start()
        return carry

    def relay(b, carry):
        for h in (0, 1):
            to = right if h == 0 else left
            for lo, n in CHUNKS:
                s2out[b, h, 16 * (1 - h):16 * (1 - h) + 16, lo:lo + n] = coded(
                    prod[b, rows_for(1 - h, to), lo:lo + n]
                )
        for h in (0, 1):
            to = right if h == 0 else left
            first_hop(b, h).wait_recv()
            for lo, n in CHUNKS:
                s2out[b, h, 16 * h:16 * h + 16, lo:lo + n] = coded(
                    prod[b, rows_for(h, to), lo:lo + n] + decoded(s1in[b, h, :, lo:lo + n])
                )
            second_hop(b, h).start()
        return carry

    def collect(b, carry):
        s = (b + 1) // 2
        block = (z + s * (1 - 2 * (b % 2)) + NZ) % NZ
        second_hop(b, 0).wait_recv()
        second_hop(b, 1).wait_recv()
        for h in (0, 1):
            rows = slice(16 * h, 16 * h + 16)
            best = None
            for lo, n in CHUNKS:
                logits = prod[b, rows_for(h, x), lo:lo + n] + (
                    decoded(s2in[b, 0, rows, lo:lo + n]) + decoded(s2in[b, 1, rows, lo:lo + n])
                )
                acc[block, rows, lo:lo + n] = logits
                part = lane_max(logits)
                best = part if best is None else jnp.maximum(best, part)
            col[block, rows, :] = best
        return carry

    def pair(i, carry):
        for s in (1, 2, 3, 4):
            @pl.when(i == s)
            def _():
                for direction in (0, 1):
                    along_z(direction, s).wait_recv()
                    if s < 4:
                        along_z(direction, s + 1).start()
                        to_sibling(2 * s - 1 + direction).start()
                if s == 4:
                    to_sibling(7).start()

        lo, hi = jnp.maximum(2 * i - 1, 0), jnp.minimum(2 * i + 1, NZ)
        lax.fori_loop(lo, hi, multiply, 0)
        lax.fori_loop(lo, hi, relay, 0)
        lax.fori_loop(jnp.maximum(2 * i - 3, 0), jnp.minimum(lo, NZ), collect, 0)
        return carry

    lax.fori_loop(0, NZ // 2 + 2, pair, 0)

    def exchanged(phase, row, combine, meanwhile):
        exc[phase, 0] = row
        sibling = remote(
            exc.at[phase, 0], exc.at[phase, 1], ecs_sem.at[phase], ecr_sem.at[phase], at(dc=1)
        )
        sibling.start()
        sibling.wait_recv()
        exn[phase, 0] = combine(row, exc[phase, 1])
        copies = []
        for k, (dy, dz) in enumerate(FAR):
            copies.append(remote(
                exn.at[phase, 0], exn.at[phase, k + 1], ens_sem.at[phase, k], enr_sem.at[phase],
                at(dy=dy, dz=dz),
            ))
            copies[-1].start()
        meanwhile()
        arrived = exn.at[phase, pl.ds(1, len(FAR))]
        remote(arrived, arrived, ens_sem.at[phase, 0], enr_sem.at[phase], at(dz=1)).wait_recv()
        row = exn[phase, 0]
        for k in range(len(FAR)):
            row = combine(row, exn[phase, k + 1])
        return row, [sibling] + copies

    def transposed():
        for g in (0, 1):
            for lo in range(0, COLS, 128):
                n = min(128, COLS - lo)
                tile = acc[4 * g:4 * g + 4, :, lo:lo + n].reshape(128, n)
                logits_t[lo:lo + n, 128 * g:128 * g + 128] = jnp.transpose(tile)

    best = jnp.max(jnp.transpose(col[...].reshape(OWNED, 128)), axis=0, keepdims=True)
    top, sent = exchanged(0, best, jnp.maximum, transposed)

    cut = math.exp(-sharpness * minp_offset)

    def kept(v):
        a = jnp.exp(v - top)
        a4 = (a * a) * (a * a)
        return (a4 * a) / (a4 + cut)

    def add_rows(k, total):
        mass = kept(logits_t[pl.ds(pl.multiple_of(k * STEP, 8), STEP), :])
        return total + jnp.sum(mass.reshape(STEP // 8, 8, OWNED), axis=0)

    total = lax.fori_loop(0, TAIL // STEP, add_rows, jnp.zeros((8, OWNED), jnp.float32))
    total = jnp.sum(total, axis=0, keepdims=True) + jnp.sum(
        kept(logits_t[TAIL:COLS, :]), axis=0, keepdims=True
    )

    def filtered(v):
        shifted = v - top
        u = sharpness * (shifted + minp_offset)
        return shifted + (jnp.minimum(u, 0.0) - jnp.log1p(jnp.exp(-jnp.abs(u))))

    def filter_all():
        def rows(k, carry):
            here = pl.ds(pl.multiple_of(k * STEP, 8), STEP)
            gated[here, :] = filtered(logits_t[here, :])
            return carry

        lax.fori_loop(0, TAIL // STEP, rows, 0)
        gated[TAIL:COLS, :] = filtered(logits_t[TAIL:COLS, :])
        pltpu.make_async_copy(gated, gated_out, o_sem).start()

    total, more = exchanged(1, total, jnp.add, filter_all)
    lnt_out[...] = jnp.log(total)

    for copy in x_copies + sent + more:
        copy.wait_send()
    for direction in (0, 1):
        for s in (1, 2, 3, 4):
            along_z(direction, s).wait_send()

    def settle(b, carry):
        to_sibling(b).wait_send()
        for h in (0, 1):
            first_hop(b, h).wait_send()
            second_hop(b, h).wait_send()
        return carry

    lax.fori_loop(0, NZ, settle, 0)
    pltpu.make_async_copy(gated, gated_out, o_sem).wait()


def body(states, head):
    dma = pltpu.SemaphoreType.DMA
    f32, bf16 = jnp.float32, jnp.bfloat16
    gated, lnt = pl.pallas_call(
        kernel,
        out_shape=(
            jax.ShapeDtypeStruct((COLS, OWNED), f32),
            jax.ShapeDtypeStruct((1, OWNED), f32),
        ),
        in_specs=[pl.BlockSpec(memory_space=pl.ANY)] * 2,
        out_specs=(
            pl.BlockSpec(memory_space=pl.ANY),
            pl.BlockSpec(memory_space=pltpu.VMEM),
        ),
        scratch_shapes=[
            pltpu.VMEM((COLS, DEPTH), bf16),
            pltpu.VMEM((DEPTH, COLS), bf16),
            pltpu.VMEM((NY * NX, LOCAL, DEPTH), bf16),
            pltpu.VMEM((NZ, BLOCK, DEPTH), bf16),
            pltpu.VMEM((NZ, BLOCK, COLS), f32),
            pltpu.VMEM((NZ, 2, PIECE, COLS), bf16),
            pltpu.VMEM((NZ, 2, PIECE, COLS), bf16),
            pltpu.VMEM((NZ, 2, 2 * PIECE, COLS), bf16),
            pltpu.VMEM((NZ, 2, 2 * PIECE, COLS), bf16),
            pltpu.VMEM((NZ, 32, COLS), f32),
            pltpu.VMEM((COLS, OWNED), f32),
            pltpu.VMEM((COLS, OWNED), f32),
            pltpu.VMEM((NZ, 32, 128), f32),
            pltpu.VMEM((2, 2, 1, OWNED), f32),
            pltpu.VMEM((2, len(FAR) + 1, 1, OWNED), f32),
            dma,
            dma,
            dma((len(PLANE),)), dma((len(PLANE),)),
            dma((2, 5)), dma((2, 5)),
            dma((NZ,)), dma((NZ,)),
            dma((NZ, 2)), dma((NZ, 2)),
            dma((NZ, 2)), dma((NZ, 2)),
            dma((2,)), dma((2,)),
            dma((2, len(FAR))), dma((2,)),
            dma,
        ],
        compiler_params=pltpu.CompilerParams(
            collective_id=0, has_side_effects=True, vmem_limit_bytes=56 * 1024 * 1024
        ),
        name="minp",
    )(states, head.T)
    return jnp.maximum(gated - lnt, -logp_floor).T


def solution(mesh):
    torus = Mesh(
        mesh.devices.reshape(NY, NZ, NC, NX),
        ("y", "z", "c", "x"),
    )
    return jax.shard_map(
        body,
        mesh=torus,
        in_specs=(P(VOCAB_HIDDEN, None), P("x", VOCAB)),
        out_specs=P("x", VOCAB),
        check_vma=False,
    )
```

```python
import math

import jax
import jax.numpy as jnp
from jax import lax
from jax.experimental import pallas as pl
from jax.experimental.pallas import tpu as pltpu
from jax.sharding import Mesh
from jax.sharding import PartitionSpec as P

MESH = pl.DeviceIdType.MESH
VOCAB = ("y", "z", "c")
VOCAB_HIDDEN = ("y", "z", "c", "x")
NX, NY, NZ, NC = 4, 4, 8, 2

sharpness = 4.0
minp_offset = math.log(10.0)
logp_floor = 30.0

BLOCK = 128
HALF = 64
SHARE = 32
PIECE = 16
LOCAL = 4
OWNED = 256
DEPTH = 1792
COLS = 2020
CHUNKS = ((0, 512), (512, 512), (1024, 512), (1536, 484))
POWER = 7
STEP = 224
TAIL = 9 * STEP

PLANE = [(dy, dx) for dy in range(NY) for dx in range(NX)]
PLANE.sort(key=lambda p: -(min(p[0], NY - p[0]) + min(p[1], NX - p[1])))
FAR = [(dy, dz) for dy in range(NY) for dz in range(NZ) if dy or dz]
FAR.sort(key=lambda p: -(min(p[0], NY - p[0]) + min(p[1], NZ - p[1])))


def coded(v):
    v2 = v * v
    v3 = v2 * v
    return (v3 * (v2 * v2)).astype(jnp.bfloat16)


def decoded(w):
    w = w.astype(jnp.float32)
    r = jnp.exp2(jnp.log2(jnp.abs(w)) * (1.0 / POWER))
    return jnp.where(w < 0.0, -r, r)


def lane_max(v):
    n = v.shape[1]
    best = v[:, 0:128]
    for lo in range(128, n, 128):
        part = v[:, lo:min(lo + 128, n)]
        if part.shape[1] < 128:
            fill = jnp.full((v.shape[0], 128 - part.shape[1]), -jnp.inf, v.dtype)
            part = jnp.concatenate([part, fill], axis=1)
        best = jnp.maximum(best, part)
    return best


def kernel(
    states, head, gated_out, lnt_out,
    raw, weights, xin, st, prod, s1out, s1in, s2out, s2in, acc, logits_t, gated, col, exc, exn,
    w_sem, xl_sem, xs_sem, xr_sem, zs_sem, zr_sem, cs_sem, cr_sem,
    s1s_sem, s1r_sem, s2s_sem, s2r_sem, ecs_sem, ecr_sem, ens_sem, enr_sem, o_sem,
):
    x, y, z, c = (lax.axis_index(n) for n in ("x", "y", "z", "c"))

    def at(dy=0, dz=0, dx=0, dc=0):
        return (
            (y + dy) % NY if dy else y,
            (z + dz) % NZ if dz else z,
            1 - c if dc else c,
            (x + dx) % NX if dx else x,
        )

    def remote(src, dst, send, recv, device):
        return pltpu.make_async_remote_copy(
            src_ref=src, dst_ref=dst, send_sem=send, recv_sem=recv,
            device_id=device, device_id_type=MESH,
        )

    w_copy = pltpu.make_async_copy(head, raw, w_sem)
    w_copy.start()
    keeper = y // 2
    slot = (y % 2) * 8 + c * NX + x
    stays = keeper == c

    barrier = pltpu.get_barrier_semaphore()

    def greet(device):
        pl.semaphore_signal(barrier, inc=1, device_id=device, device_id_type=MESH)

    for dx in range(NX):
        for j in range(2):
            for cc in range(NC):
                sender = (2 * c + j, z, cc, (x + dx) % NX)
                if dx:
                    greet(sender)
                else:
                    @pl.when(jnp.logical_or(2 * c + j != y, cc != c))
                    def _():
                        greet(sender)
    for device in (at(dz=1), at(dz=NZ - 1), at(dc=1)):
        greet(device)
    pl.semaphore_wait(barrier, 19 - stays.astype(jnp.int32))

    def piece(k, dy, dx):
        to = (x + dx) % NX
        return remote(
            states.at[:, pl.ds(pl.multiple_of(to * DEPTH, 128), DEPTH)], xin.at[slot],
            xs_sem.at[k], xr_sem.at[slot], ((y + dy) % NY, z, keeper, to),
        )

    own_piece = pltpu.make_async_copy(
        states.at[:, pl.ds(pl.multiple_of(x * DEPTH, 128), DEPTH)], xin.at[slot], xl_sem
    )
    for k, (dy, dx) in enumerate(PLANE):
        if dy or dx:
            piece(k, dy, dx).start()
        else:
            pl.when(jnp.logical_not(stays))(lambda: piece(k, 0, 0).start())
            pl.when(stays)(own_piece.start)

    w_copy.wait()
    for lo in range(0, COLS, 256):
        n = min(256, COLS - lo)
        weights[:, lo:lo + n] = jnp.transpose(raw[lo:lo + n, :])

    pl.when(stays)(own_piece.wait)
    for k in range(4 * NX):
        arrived = remote(xin.at[k], xin.at[k], xs_sem.at[k], xr_sem.at[k], at(dc=1))
        pl.when(jnp.logical_or(jnp.logical_not(stays), k != slot))(arrived.wait_recv)
    for j in range(2):
        for cc in range(NC):
            pieces = [xin[j * 8 + cc * NX + k].astype(jnp.float32) for k in range(NX)]
            rows = pl.ds(pl.multiple_of(cc * HALF + c * SHARE + j * PIECE, PIECE), PIECE)
            st[0, rows, :] = jnp.concatenate(pieces, axis=0).astype(jnp.bfloat16)

    def share(b, h):
        return st.at[b, pl.ds(pl.multiple_of(h * HALF + c * SHARE, SHARE), SHARE), :]

    def along_z(source, source_h, target, target_h, way):
        return remote(
            share(source, source_h), share(target, target_h),
            zs_sem.at[target, target_h], zr_sem.at[target, target_h],
            (y, (z + 1 - 2 * way + NZ) % NZ, c, x),
        )

    def to_sibling(b, h):
        return remote(share(b, h), share(b, h), cs_sem.at[b, h], cr_sem.at[b, h], at(dc=1))

    for h in (0, 1):
        to_sibling(0, h).start()
    for p in (0, 1):
        for way in (0, 1):
            along_z(0, p, 1 + p, way, way).start()

    right, left, across = (x + 1) % NX, (x + NX - 1) % NX, (x + 2) % NX

    def first_hop(b, h):
        return remote(
            s1out.at[b, h], s1in.at[b, h], s1s_sem.at[b, h], s1r_sem.at[b, h],
            at(dx=1 if h == 0 else NX - 1),
        )

    def second_hop(b, h):
        return remote(
            s2out.at[b, h], s2in.at[b, h], s2s_sem.at[b, h], s2r_sem.at[b, h],
            at(dx=1 if h == 0 else NX - 1),
        )

    def rows_for(h, d):
        return pl.ds(pl.multiple_of(h * HALF + d * PIECE, PIECE), PIECE)

    def multiply(b):
        for h in (0, 1):
            to_sibling(b, h).wait_recv()
        for lo, n in CHUNKS:
            prod[b, :, lo:lo + n] = jnp.dot(
                st[b], weights[:, lo:lo + n], preferred_element_type=jnp.float32
            )
        for h in (0, 1):
            for lo, n in CHUNKS:
                s1out[b, h, :, lo:lo + n] = coded(prod[b, rows_for(h, across), lo:lo + n])
            first_hop(b, h).start()

    def relay(b):
        for h in (0, 1):
            to = right if h == 0 else left
            for lo, n in CHUNKS:
                s2out[b, h, 16 * (1 - h):16 * (1 - h) + 16, lo:lo + n] = coded(
                    prod[b, rows_for(1 - h, to), lo:lo + n]
                )
        for h in (0, 1):
            to = right if h == 0 else left
            first_hop(b, h).wait_recv()
            for lo, n in CHUNKS:
                s2out[b, h, 16 * h:16 * h + 16, lo:lo + n] = coded(
                    prod[b, rows_for(h, to), lo:lo + n] + decoded(s1in[b, h, :, lo:lo + n])
                )
            second_hop(b, h).start()

    def collect(b):
        alone = jnp.logical_or(b == 0, b == NZ - 1)
        s = (b + 1) // 2
        second_hop(b, 0).wait_recv()
        second_hop(b, 1).wait_recv()
        for h in (0, 1):
            rows = slice(16 * h, 16 * h + 16)
            block = jnp.where(alone, z + s, z + NZ + (2 * h - 1) * s) % NZ
            core = jnp.where(alone, h, 1 - b % 2)
            mine = pl.ds(pl.multiple_of(core * PIECE, PIECE), PIECE)
            best = None
            for lo, n in CHUNKS:
                logits = prod[b, rows_for(h, x), lo:lo + n] + (
                    decoded(s2in[b, 0, rows, lo:lo + n]) + decoded(s2in[b, 1, rows, lo:lo + n])
                )
                acc[block, mine, lo:lo + n] = logits
                part = lane_max(logits)
                best = part if best is None else jnp.maximum(best, part)
            col[block, mine, :] = best

    def pass_on(b):
        for h in (0, 1):
            along_z(b, h, b, h, h).wait_recv()

            @pl.when(b <= 4)
            def _():
                along_z(b, h, b + 2, h, h).start()

            to_sibling(b, h).start()

        @pl.when(jnp.logical_or(b == 5, b == 6))
        def _():
            p = 1 - b % 2
            along_z(b, p, 7, p, p).start()

    def step(b, carry):
        pl.when(b < NZ)(lambda: multiply(b))
        pl.when(b < NZ - 1)(lambda: pass_on(b + 1))
        pl.when(jnp.logical_and(b != 1, b <= NZ))(lambda: relay(jnp.maximum(b - 1, 0)))
        pl.when(b >= 3)(lambda: collect(b - 3))
        return carry

    lax.fori_loop(0, NZ + 3, step, 0)

    def exchanged(phase, row, combine, meanwhile):
        exc[phase, 0] = row
        sibling = remote(
            exc.at[phase, 0], exc.at[phase, 1], ecs_sem.at[phase], ecr_sem.at[phase], at(dc=1)
        )
        sibling.start()
        sibling.wait_recv()
        exn[phase, 0] = combine(row, exc[phase, 1])
        copies = []
        for k, (dy, dz) in enumerate(FAR):
            copies.append(remote(
                exn.at[phase, 0], exn.at[phase, k + 1], ens_sem.at[phase, k], enr_sem.at[phase],
                at(dy=dy, dz=dz),
            ))
            copies[-1].start()
        meanwhile()
        arrived = exn.at[phase, pl.ds(1, len(FAR))]
        remote(arrived, arrived, ens_sem.at[phase, 0], enr_sem.at[phase], at(dz=1)).wait_recv()
        row = exn[phase, 0]
        for k in range(len(FAR)):
            row = combine(row, exn[phase, k + 1])
        return row, [sibling] + copies

    def transposed():
        for g in (0, 1):
            for lo in range(0, COLS, 128):
                n = min(128, COLS - lo)
                tile = acc[4 * g:4 * g + 4, :, lo:lo + n].reshape(128, n)
                logits_t[lo:lo + n, 128 * g:128 * g + 128] = jnp.transpose(tile)

    best = jnp.max(jnp.transpose(col[...].reshape(OWNED, 128)), axis=0, keepdims=True)
    top, sent = exchanged(0, best, jnp.maximum, transposed)

    cut = math.exp(-sharpness * minp_offset)

    def kept(v):
        a = jnp.exp(v - top)
        a4 = (a * a) * (a * a)
        return (a4 * a) / (a4 + cut)

    def add_rows(k, total):
        mass = kept(logits_t[pl.ds(pl.multiple_of(k * STEP, 8), STEP), :])
        return total + jnp.sum(mass.reshape(STEP // 8, 8, OWNED), axis=0)

    total = lax.fori_loop(0, TAIL // STEP, add_rows, jnp.zeros((8, OWNED), jnp.float32))
    total = jnp.sum(total, axis=0, keepdims=True) + jnp.sum(
        kept(logits_t[TAIL:COLS, :]), axis=0, keepdims=True
    )

    def filtered(v):
        shifted = v - top
        u = sharpness * (shifted + minp_offset)
        return shifted + (jnp.minimum(u, 0.0) - jnp.log1p(jnp.exp(-jnp.abs(u))))

    def filter_all():
        def rows(k, carry):
            here = pl.ds(pl.multiple_of(k * STEP, 8), STEP)
            gated[here, :] = filtered(logits_t[here, :])
            return carry

        lax.fori_loop(0, TAIL // STEP, rows, 0)
        gated[TAIL:COLS, :] = filtered(logits_t[TAIL:COLS, :])
        pltpu.make_async_copy(gated, gated_out, o_sem).start()

    total, more = exchanged(1, total, jnp.add, filter_all)
    lnt_out[...] = jnp.log(total)

    for k, (dy, dx) in enumerate(PLANE):
        if dy or dx:
            piece(k, dy, dx).wait_send()
        else:
            pl.when(jnp.logical_not(stays))(lambda: piece(k, 0, 0).wait_send())
    for copy in sent + more:
        copy.wait_send()

    def settle(b, carry):
        for h in (0, 1):
            pl.when(b >= 1)(along_z(b, h, b, h, h).wait_send)
            to_sibling(b, h).wait_send()
            first_hop(b, h).wait_send()
            second_hop(b, h).wait_send()
        return carry

    lax.fori_loop(0, NZ, settle, 0)
    pltpu.make_async_copy(gated, gated_out, o_sem).wait()


def body(states, head):
    dma = pltpu.SemaphoreType.DMA
    f32, bf16 = jnp.float32, jnp.bfloat16
    gated, lnt = pl.pallas_call(
        kernel,
        out_shape=(
            jax.ShapeDtypeStruct((COLS, OWNED), f32),
            jax.ShapeDtypeStruct((1, OWNED), f32),
        ),
        in_specs=[pl.BlockSpec(memory_space=pl.ANY)] * 2,
        out_specs=(
            pl.BlockSpec(memory_space=pl.ANY),
            pl.BlockSpec(memory_space=pltpu.VMEM),
        ),
        scratch_shapes=[
            pltpu.VMEM((COLS, DEPTH), bf16),
            pltpu.VMEM((DEPTH, COLS), bf16),
            pltpu.VMEM((NY * NX, LOCAL, DEPTH), bf16),
            pltpu.VMEM((NZ, BLOCK, DEPTH), bf16),
            pltpu.VMEM((NZ, BLOCK, COLS), f32),
            pltpu.VMEM((NZ, 2, PIECE, COLS), bf16),
            pltpu.VMEM((NZ, 2, PIECE, COLS), bf16),
            pltpu.VMEM((NZ, 2, 2 * PIECE, COLS), bf16),
            pltpu.VMEM((NZ, 2, 2 * PIECE, COLS), bf16),
            pltpu.VMEM((NZ, 32, COLS), f32),
            pltpu.VMEM((COLS, OWNED), f32),
            pltpu.VMEM((COLS, OWNED), f32),
            pltpu.VMEM((NZ, 32, 128), f32),
            pltpu.VMEM((2, 2, 1, OWNED), f32),
            pltpu.VMEM((2, len(FAR) + 1, 1, OWNED), f32),
            dma,
            dma,
            dma((len(PLANE),)), dma((len(PLANE),)),
            dma((NZ, 2)), dma((NZ, 2)),
            dma((NZ, 2)), dma((NZ, 2)),
            dma((NZ, 2)), dma((NZ, 2)),
            dma((NZ, 2)), dma((NZ, 2)),
            dma((2,)), dma((2,)),
            dma((2, len(FAR))), dma((2,)),
            dma,
        ],
        compiler_params=pltpu.CompilerParams(
            collective_id=0, has_side_effects=True, vmem_limit_bytes=56 * 1024 * 1024
        ),
        name="minp",
    )(states, head.T)
    return jnp.maximum(gated - lnt, -logp_floor).T


def solution(mesh):
    torus = Mesh(
        mesh.devices.reshape(NY, NZ, NC, NX),
        ("y", "z", "c", "x"),
    )
    return jax.shard_map(
        body,
        mesh=torus,
        in_specs=(P(VOCAB_HIDDEN, None), P("x", VOCAB)),
        out_specs=P("x", VOCAB),
        check_vma=False,
    )
```

```python
import math

import jax
import jax.numpy as jnp
from jax import lax
from jax.experimental import pallas as pl
from jax.experimental.pallas import tpu as pltpu
from jax.sharding import Mesh
from jax.sharding import PartitionSpec as P

MESH = pl.DeviceIdType.MESH
VOCAB = ("y", "z", "c")
VOCAB_HIDDEN = ("y", "z", "c", "x")
NX, NY, NZ, NC = 4, 4, 8, 2

sharpness = 4.0
minp_offset = math.log(10.0)
logp_floor = 30.0

BLOCK = 128
HALF = 64
SHARE = 32
PIECE = 16
LOCAL = 4
OWNED = 256
DEPTH = 1792
COLS = 2020
CHUNKS = ((0, 512), (512, 512), (1024, 512), (1536, 484))
POWER = 7
STEP = 224
TAIL = 9 * STEP

PLANE = [(dy, dx) for dy in range(NY) for dx in range(NX)]
PLANE.sort(key=lambda p: -(min(p[0], NY - p[0]) + min(p[1], NX - p[1])))
FAR = [(dy, dz) for dy in range(NY) for dz in range(NZ) if dy or dz]
FAR.sort(key=lambda p: -(min(p[0], NY - p[0]) + min(p[1], NZ - p[1])))


def coded(v):
    v2 = v * v
    v3 = v2 * v
    return (v3 * (v2 * v2)).astype(jnp.bfloat16)


def decoded(w):
    w = w.astype(jnp.float32)
    r = jnp.exp2(jnp.log2(jnp.abs(w)) * (1.0 / POWER))
    return jnp.where(w < 0.0, -r, r)


def lane_max(v):
    n = v.shape[1]
    best = v[:, 0:128]
    for lo in range(128, n, 128):
        part = v[:, lo:min(lo + 128, n)]
        if part.shape[1] < 128:
            fill = jnp.full((v.shape[0], 128 - part.shape[1]), -jnp.inf, v.dtype)
            part = jnp.concatenate([part, fill], axis=1)
        best = jnp.maximum(best, part)
    return best


def kernel(
    states, head, gated, lnt_out,
    raw, weights, xin, st, prod, s1out, s1in, s2out, s2in, acc, logits_t, col, exc, exn,
    w_sem, xl_sem, xs_sem, xr_sem, zs_sem, zr_sem, cs_sem, cr_sem,
    s1s_sem, s1r_sem, s2s_sem, s2r_sem, ecs_sem, ecr_sem, ens_sem, enr_sem,
):
    x, y, z, c = (lax.axis_index(n) for n in ("x", "y", "z", "c"))

    def at(dy=0, dz=0, dx=0, dc=0):
        return (
            (y + dy) % NY if dy else y,
            (z + dz) % NZ if dz else z,
            1 - c if dc else c,
            (x + dx) % NX if dx else x,
        )

    def remote(src, dst, send, recv, device):
        return pltpu.make_async_remote_copy(
            src_ref=src, dst_ref=dst, send_sem=send, recv_sem=recv,
            device_id=device, device_id_type=MESH,
        )

    w_copy = pltpu.make_async_copy(head, raw, w_sem)
    w_copy.start()
    keeper = y // 2
    slot = (y % 2) * 8 + c * NX + x
    stays = keeper == c

    barrier = pltpu.get_barrier_semaphore()

    def greet(device):
        pl.semaphore_signal(barrier, inc=1, device_id=device, device_id_type=MESH)

    for dx in range(NX):
        for j in range(2):
            for cc in range(NC):
                sender = (2 * c + j, z, cc, (x + dx) % NX)
                if dx:
                    greet(sender)
                else:
                    @pl.when(jnp.logical_or(2 * c + j != y, cc != c))
                    def _():
                        greet(sender)
    for device in (at(dz=1), at(dz=NZ - 1), at(dc=1)):
        greet(device)
    pl.semaphore_wait(barrier, 19 - stays.astype(jnp.int32))

    def piece(k, dy, dx):
        to = (x + dx) % NX
        return remote(
            states.at[:, pl.ds(pl.multiple_of(to * DEPTH, 128), DEPTH)], xin.at[slot],
            xs_sem.at[k], xr_sem.at[slot], ((y + dy) % NY, z, keeper, to),
        )

    own_piece = pltpu.make_async_copy(
        states.at[:, pl.ds(pl.multiple_of(x * DEPTH, 128), DEPTH)], xin.at[slot], xl_sem
    )
    for k, (dy, dx) in enumerate(PLANE):
        if dy or dx:
            piece(k, dy, dx).start()
        else:
            pl.when(jnp.logical_not(stays))(lambda: piece(k, 0, 0).start())
            pl.when(stays)(own_piece.start)

    w_copy.wait()
    for lo in range(0, COLS, 256):
        n = min(256, COLS - lo)
        weights[:, lo:lo + n] = jnp.transpose(raw[lo:lo + n, :])

    pl.when(stays)(own_piece.wait)
    for k in range(4 * NX):
        arrived = remote(xin.at[k], xin.at[k], xs_sem.at[k], xr_sem.at[k], at(dc=1))
        pl.when(jnp.logical_or(jnp.logical_not(stays), k != slot))(arrived.wait_recv)
    for j in range(2):
        for cc in range(NC):
            pieces = [xin[j * 8 + cc * NX + k].astype(jnp.float32) for k in range(NX)]
            rows = pl.ds(pl.multiple_of(cc * HALF + c * SHARE + j * PIECE, PIECE), PIECE)
            st[0, rows, :] = jnp.concatenate(pieces, axis=0).astype(jnp.bfloat16)

    def share(b, h):
        return st.at[b, pl.ds(pl.multiple_of(h * HALF + c * SHARE, SHARE), SHARE), :]

    def along_z(source, source_h, target, target_h, way):
        return remote(
            share(source, source_h), share(target, target_h),
            zs_sem.at[target, target_h], zr_sem.at[target, target_h],
            (y, (z + 1 - 2 * way + NZ) % NZ, c, x),
        )

    def to_sibling(b, h):
        return remote(share(b, h), share(b, h), cs_sem.at[b, h], cr_sem.at[b, h], at(dc=1))

    for h in (0, 1):
        to_sibling(0, h).start()
    for p in (0, 1):
        for way in (0, 1):
            along_z(0, p, 1 + p, way, way).start()

    right, left, across = (x + 1) % NX, (x + NX - 1) % NX, (x + 2) % NX

    def first_hop(b, h):
        return remote(
            s1out.at[b, h], s1in.at[b, h], s1s_sem.at[b, h], s1r_sem.at[b, h],
            at(dx=1 if h == 0 else NX - 1),
        )

    def second_hop(b, h):
        return remote(
            s2out.at[b, h], s2in.at[b, h], s2s_sem.at[b, h], s2r_sem.at[b, h],
            at(dx=1 if h == 0 else NX - 1),
        )

    def rows_for(h, d):
        return pl.ds(pl.multiple_of(h * HALF + d * PIECE, PIECE), PIECE)

    def multiply(b):
        for h in (0, 1):
            to_sibling(b, h).wait_recv()
        for lo, n in CHUNKS:
            prod[b, :, lo:lo + n] = jnp.dot(
                st[b], weights[:, lo:lo + n], preferred_element_type=jnp.float32
            )
        for h in (0, 1):
            for lo, n in CHUNKS:
                s1out[b, h, :, lo:lo + n] = coded(prod[b, rows_for(h, across), lo:lo + n])
            first_hop(b, h).start()

    def relay(b):
        for h in (0, 1):
            to = right if h == 0 else left
            for lo, n in CHUNKS:
                s2out[b, h, 16 * (1 - h):16 * (1 - h) + 16, lo:lo + n] = coded(
                    prod[b, rows_for(1 - h, to), lo:lo + n]
                )
        for h in (0, 1):
            to = right if h == 0 else left
            first_hop(b, h).wait_recv()
            for lo, n in CHUNKS:
                s2out[b, h, 16 * h:16 * h + 16, lo:lo + n] = coded(
                    prod[b, rows_for(h, to), lo:lo + n] + decoded(s1in[b, h, :, lo:lo + n])
                )
            second_hop(b, h).start()

    def collect(b):
        alone = jnp.logical_or(b == 0, b == NZ - 1)
        s = (b + 1) // 2
        second_hop(b, 0).wait_recv()
        second_hop(b, 1).wait_recv()
        for h in (0, 1):
            rows = slice(16 * h, 16 * h + 16)
            block = jnp.where(alone, z + s, z + NZ + (2 * h - 1) * s) % NZ
            core = jnp.where(alone, h, 1 - b % 2)
            mine = pl.ds(pl.multiple_of(core * PIECE, PIECE), PIECE)
            best = None
            for lo, n in CHUNKS:
                logits = prod[b, rows_for(h, x), lo:lo + n] + (
                    decoded(s2in[b, 0, rows, lo:lo + n]) + decoded(s2in[b, 1, rows, lo:lo + n])
                )
                acc[block, mine, lo:lo + n] = logits
                part = lane_max(logits)
                best = part if best is None else jnp.maximum(best, part)
            col[block, mine, :] = best

    def pass_on(b):
        for h in (0, 1):
            along_z(b, h, b, h, h).wait_recv()

            @pl.when(b <= 4)
            def _():
                along_z(b, h, b + 2, h, h).start()

            to_sibling(b, h).start()

        @pl.when(jnp.logical_or(b == 5, b == 6))
        def _():
            p = 1 - b % 2
            along_z(b, p, 7, p, p).start()

    def step(b, carry):
        pl.when(b < NZ)(lambda: multiply(b))
        pl.when(b < NZ - 1)(lambda: pass_on(b + 1))
        pl.when(jnp.logical_and(b != 1, b <= NZ))(lambda: relay(jnp.maximum(b - 1, 0)))
        pl.when(b >= 3)(lambda: collect(b - 3))
        return carry

    lax.fori_loop(0, NZ + 3, step, 0)

    def exchanged(phase, row, combine, meanwhile):
        exc[phase, 0] = row
        sibling = remote(
            exc.at[phase, 0], exc.at[phase, 1], ecs_sem.at[phase], ecr_sem.at[phase], at(dc=1)
        )
        sibling.start()
        sibling.wait_recv()
        exn[phase, 0] = combine(row, exc[phase, 1])
        for k, (dy, dz) in enumerate(FAR):
            remote(
                exn.at[phase, 0], exn.at[phase, k + 1], ens_sem.at[phase], enr_sem.at[phase],
                at(dy=dy, dz=dz),
            ).start()
        meanwhile()
        arrived = exn.at[phase, pl.ds(1, len(FAR))]
        everyone = remote(arrived, arrived, ens_sem.at[phase], enr_sem.at[phase], at(dz=1))
        sibling.wait_send()
        everyone.wait_recv()
        row = exn[phase, 0]
        for k in range(len(FAR)):
            row = combine(row, exn[phase, k + 1])
        return row, everyone

    def settle(b, carry):
        for h in (0, 1):
            pl.when(b >= 1)(along_z(b, h, b, h, h).wait_send)
            to_sibling(b, h).wait_send()
            first_hop(b, h).wait_send()
            second_hop(b, h).wait_send()
        return carry

    def transposed():
        for k, (dy, dx) in enumerate(PLANE):
            if dy or dx:
                piece(k, dy, dx).wait_send()
            else:
                pl.when(jnp.logical_not(stays))(lambda: piece(k, 0, 0).wait_send())
        lax.fori_loop(0, NZ, settle, 0)
        for g in (0, 1):
            for lo in range(0, COLS, 128):
                n = min(128, COLS - lo)
                tile = acc[4 * g:4 * g + 4, :, lo:lo + n].reshape(128, n)
                logits_t[lo:lo + n, 128 * g:128 * g + 128] = jnp.transpose(tile)

    best = jnp.max(jnp.transpose(col[...].reshape(OWNED, 128)), axis=0, keepdims=True)
    top, sent_top = exchanged(0, best, jnp.maximum, transposed)

    cut = math.exp(-sharpness * minp_offset)

    def kept(v):
        a = jnp.exp(v - top)
        a4 = (a * a) * (a * a)
        return (a4 * a) / (a4 + cut)

    def add_rows(k, total):
        mass = kept(logits_t[pl.ds(pl.multiple_of(k * STEP, 8), STEP), :])
        return total + jnp.sum(mass.reshape(STEP // 8, 8, OWNED), axis=0)

    total = lax.fori_loop(0, TAIL // STEP, add_rows, jnp.zeros((8, OWNED), jnp.float32))
    total = jnp.sum(total, axis=0, keepdims=True) + jnp.sum(
        kept(logits_t[TAIL:COLS, :]), axis=0, keepdims=True
    )

    def filtered(v):
        shifted = v - top
        u = sharpness * (shifted + minp_offset)
        return shifted + (jnp.minimum(u, 0.0) - jnp.log1p(jnp.exp(-jnp.abs(u))))

    def filter_all():
        def rows(k, carry):
            here = pl.ds(pl.multiple_of(k * STEP, 8), STEP)
            gated[here, :] = filtered(logits_t[here, :])
            return carry

        lax.fori_loop(0, TAIL // STEP, rows, 0)
        gated[TAIL:COLS, :] = filtered(logits_t[TAIL:COLS, :])

    total, sent_total = exchanged(1, total, jnp.add, filter_all)
    lnt_out[...] = jnp.log(total)

    sent_top.wait_send()
    sent_total.wait_send()


def body(states, head):
    dma = pltpu.SemaphoreType.DMA
    f32, bf16 = jnp.float32, jnp.bfloat16
    gated, lnt = pl.pallas_call(
        kernel,
        out_shape=(
            jax.ShapeDtypeStruct((COLS, OWNED), f32),
            jax.ShapeDtypeStruct((1, OWNED), f32),
        ),
        in_specs=[pl.BlockSpec(memory_space=pltpu.HBM)] * 2,
        out_specs=(pl.BlockSpec(memory_space=pltpu.VMEM),) * 2,
        scratch_shapes=[
            pltpu.VMEM((COLS, DEPTH), bf16),
            pltpu.VMEM((DEPTH, COLS), bf16),
            pltpu.VMEM((NY * NX, LOCAL, DEPTH), bf16),
            pltpu.VMEM((NZ, BLOCK, DEPTH), bf16),
            pltpu.VMEM((NZ, BLOCK, COLS), f32),
            pltpu.VMEM((NZ, 2, PIECE, COLS), bf16),
            pltpu.VMEM((NZ, 2, PIECE, COLS), bf16),
            pltpu.VMEM((NZ, 2, 2 * PIECE, COLS), bf16),
            pltpu.VMEM((NZ, 2, 2 * PIECE, COLS), bf16),
            pltpu.VMEM((NZ, 32, COLS), f32),
            pltpu.VMEM((COLS, OWNED), f32),
            pltpu.VMEM((NZ, 32, 128), f32),
            pltpu.VMEM((2, 2, 1, OWNED), f32),
            pltpu.VMEM((2, len(FAR) + 1, 1, OWNED), f32),
            dma,
            dma,
            dma((len(PLANE),)), dma((len(PLANE),)),
            dma((NZ, 2)), dma((NZ, 2)),
            dma((NZ, 2)), dma((NZ, 2)),
            dma((NZ, 2)), dma((NZ, 2)),
            dma((NZ, 2)), dma((NZ, 2)),
            dma((2,)), dma((2,)),
            dma((2,)), dma((2,)),
        ],
        compiler_params=pltpu.CompilerParams(
            collective_id=0, has_side_effects=True, vmem_limit_bytes=48 * 1024 * 1024
        ),
        name="minp",
    )(
        pltpu.with_memory_space_constraint(states, pltpu.HBM),
        pltpu.with_memory_space_constraint(head.T, pltpu.HBM),
    )
    return jnp.maximum(gated - lnt, -logp_floor).T


def solution(mesh):
    torus = Mesh(
        mesh.devices.reshape(NY, NZ, NC, NX),
        ("y", "z", "c", "x"),
    )
    return jax.shard_map(
        body,
        mesh=torus,
        in_specs=(P(VOCAB_HIDDEN, None), P("x", VOCAB)),
        out_specs=P("x", VOCAB),
        check_vma=False,
    )
```

```python
import math

import jax
import jax.numpy as jnp
from jax import lax
from jax.experimental import pallas as pl
from jax.experimental.pallas import tpu as pltpu
from jax.sharding import Mesh
from jax.sharding import PartitionSpec as P

MESH = pl.DeviceIdType.MESH
VOCAB = ("y", "z", "c")
VOCAB_HIDDEN = ("y", "z", "c", "x")
NX, NY, NZ, NC = 4, 4, 8, 2

sharpness = 4.0
minp_offset = math.log(10.0)
logp_floor = 30.0

BLOCK = 128
HALF = 64
SHARE = 32
PIECE = 16
LOCAL = 4
OWNED = 256
DEPTH = 1792
COLS = 2020
CHUNKS = ((0, 512), (512, 512), (1024, 512), (1536, 484))
POWER = 7
STEP = 224
TAIL = 9 * STEP

PLANE = [(dy, dx) for dy in range(NY) for dx in range(NX)]
PLANE.sort(key=lambda p: -(min(p[0], NY - p[0]) + min(p[1], NX - p[1])))
CHIPS = [(dy, dz) for dy in range(NY) for dz in range(NZ) if dy or dz]
AWAY = {p: min(p[0], NY - p[0]) + min(p[1], NZ - p[1]) for p in CHIPS}
CHIPS.sort(key=lambda p: -AWAY[p])
FAR = [p for p in CHIPS if AWAY[p] >= 5]
NEAR = [p for p in CHIPS if AWAY[p] < 5]
LANDED = 2 * len(FAR) + len(NEAR)


def coded(v):
    v2 = v * v
    v3 = v2 * v
    return (v3 * (v2 * v2)).astype(jnp.bfloat16)


def decoded(w):
    w = w.astype(jnp.float32)
    r = jnp.exp2(jnp.log2(jnp.abs(w)) * (1.0 / POWER))
    return jnp.where(w < 0.0, -r, r)


def lane_max(v):
    n = v.shape[1]
    best = v[:, 0:128]
    for lo in range(128, n, 128):
        part = v[:, lo:min(lo + 128, n)]
        if part.shape[1] < 128:
            fill = jnp.full((v.shape[0], 128 - part.shape[1]), -jnp.inf, v.dtype)
            part = jnp.concatenate([part, fill], axis=1)
        best = jnp.maximum(best, part)
    return best


def kernel(
    states, head, gated, lnt_out,
    raw, weights, xin, st, prod, s1out, s1in, s2out, s2in, acc, logits_t, e4, e5, col, ex,
    w_sem, xl_sem, xs_sem, xr_sem, zs_sem, zr_sem, cs_sem, cr_sem,
    s1s_sem, s1r_sem, s2s_sem, s2r_sem, es_sem, er_sem,
):
    x, y, z, c = (lax.axis_index(n) for n in ("x", "y", "z", "c"))

    def at(dy=0, dz=0, dx=0, dc=0):
        return (
            (y + dy) % NY if dy else y,
            (z + dz) % NZ if dz else z,
            1 - c if dc else c,
            (x + dx) % NX if dx else x,
        )

    def remote(src, dst, send, recv, device):
        return pltpu.make_async_remote_copy(
            src_ref=src, dst_ref=dst, send_sem=send, recv_sem=recv,
            device_id=device, device_id_type=MESH,
        )

    w_copy = pltpu.make_async_copy(head, raw, w_sem)
    w_copy.start()
    keeper = y // 2
    slot = (y % 2) * 8 + c * NX + x
    stays = keeper == c

    barrier = pltpu.get_barrier_semaphore()

    def greet(device):
        pl.semaphore_signal(barrier, inc=1, device_id=device, device_id_type=MESH)

    for dx in range(NX):
        for j in range(2):
            for cc in range(NC):
                sender = (2 * c + j, z, cc, (x + dx) % NX)
                if dx:
                    greet(sender)
                else:
                    @pl.when(jnp.logical_or(2 * c + j != y, cc != c))
                    def _():
                        greet(sender)
    for device in (at(dz=1), at(dz=NZ - 1), at(dc=1)):
        greet(device)
    pl.semaphore_wait(barrier, 19 - stays.astype(jnp.int32))

    def piece(k, dy, dx):
        to = (x + dx) % NX
        return remote(
            states.at[:, pl.ds(pl.multiple_of(to * DEPTH, 128), DEPTH)], xin.at[slot],
            xs_sem.at[k], xr_sem.at[slot], ((y + dy) % NY, z, keeper, to),
        )

    own_piece = pltpu.make_async_copy(
        states.at[:, pl.ds(pl.multiple_of(x * DEPTH, 128), DEPTH)], xin.at[slot], xl_sem
    )
    for k, (dy, dx) in enumerate(PLANE):
        if dy or dx:
            piece(k, dy, dx).start()
        else:
            pl.when(jnp.logical_not(stays))(lambda: piece(k, 0, 0).start())
            pl.when(stays)(own_piece.start)

    w_copy.wait()
    for lo in range(0, COLS, 256):
        n = min(256, COLS - lo)
        weights[:, lo:lo + n] = jnp.transpose(raw[lo:lo + n, :])

    pl.when(stays)(own_piece.wait)
    for k in range(4 * NX):
        arrived = remote(xin.at[k], xin.at[k], xs_sem.at[k], xr_sem.at[k], at(dc=1))
        pl.when(jnp.logical_or(jnp.logical_not(stays), k != slot))(arrived.wait_recv)
    for j in range(2):
        for cc in range(NC):
            pieces = [xin[j * 8 + cc * NX + k].astype(jnp.float32) for k in range(NX)]
            rows = pl.ds(pl.multiple_of(cc * HALF + c * SHARE + j * PIECE, PIECE), PIECE)
            st[0, rows, :] = jnp.concatenate(pieces, axis=0).astype(jnp.bfloat16)

    def share(b, h):
        return st.at[b, pl.ds(pl.multiple_of(h * HALF + c * SHARE, SHARE), SHARE), :]

    def along_z(source, source_h, target, target_h, way):
        return remote(
            share(source, source_h), share(target, target_h),
            zs_sem.at[target, target_h], zr_sem.at[target, target_h],
            (y, (z + 1 - 2 * way + NZ) % NZ, c, x),
        )

    def to_sibling(b, h):
        return remote(share(b, h), share(b, h), cs_sem.at[b, h], cr_sem.at[b, h], at(dc=1))

    for h in (0, 1):
        to_sibling(0, h).start()
    for p in (0, 1):
        for way in (0, 1):
            along_z(0, p, 1 + p, way, way).start()

    right, left, across = (x + 1) % NX, (x + NX - 1) % NX, (x + 2) % NX

    def first_hop(b, h):
        return remote(
            s1out.at[b, h], s1in.at[b, h], s1s_sem.at[b, h], s1r_sem.at[b, h],
            at(dx=1 if h == 0 else NX - 1),
        )

    def second_hop(b, h, part):
        return remote(
            s2out.at[b, h, part], s2in.at[b, h, part], s2s_sem.at[b, h, part], s2r_sem.at[b, h, part],
            at(dx=1 if h == 0 else NX - 1),
        )

    def rows_for(h, d):
        return pl.ds(pl.multiple_of(h * HALF + d * PIECE, PIECE), PIECE)

    def multiply(b):
        for h in (0, 1):
            to_sibling(b, h).wait_recv()
        for lo, n in CHUNKS:
            prod[b, :, lo:lo + n] = jnp.dot(
                st[b], weights[:, lo:lo + n], preferred_element_type=jnp.float32
            )
        for h in (0, 1):
            for lo, n in CHUNKS:
                s1out[b, h, :, lo:lo + n] = coded(prod[b, rows_for(h, across), lo:lo + n])
            first_hop(b, h).start()
        for h in (0, 1):
            to = right if h == 0 else left
            for lo, n in CHUNKS:
                s2out[b, h, 0, :, lo:lo + n] = coded(prod[b, rows_for(1 - h, to), lo:lo + n])
            second_hop(b, h, 0).start()

    def relay(b):
        for h in (0, 1):
            to = right if h == 0 else left
            first_hop(b, h).wait_recv()
            for lo, n in CHUNKS:
                s2out[b, h, 1, :, lo:lo + n] = coded(
                    prod[b, rows_for(h, to), lo:lo + n] + decoded(s1in[b, h, :, lo:lo + n])
                )
            second_hop(b, h, 1).start()

    def collect(b):
        alone = jnp.logical_or(b == 0, b == NZ - 1)
        s = (b + 1) // 2
        for h in (0, 1):
            second_hop(b, 1 - h, 0).wait_recv()
            second_hop(b, h, 1).wait_recv()
            block = jnp.where(alone, z + s, z + NZ + (2 * h - 1) * s) % NZ
            core = jnp.where(alone, h, 1 - b % 2)
            mine = pl.ds(pl.multiple_of(core * PIECE, PIECE), PIECE)
            best = None
            for lo, n in CHUNKS:
                logits = prod[b, rows_for(h, x), lo:lo + n] + (
                    decoded(s2in[b, h, 1, :, lo:lo + n])
                    + decoded(s2in[b, 1 - h, 0, :, lo:lo + n])
                )
                acc[block, mine, lo:lo + n] = logits
                part = lane_max(logits)
                best = part if best is None else jnp.maximum(best, part)
            col[block, mine, :] = best

    def pass_on(b):
        for h in (0, 1):
            along_z(b, h, b, h, h).wait_recv()

            @pl.when(b <= 4)
            def _():
                along_z(b, h, b + 2, h, h).start()

            to_sibling(b, h).start()

        @pl.when(jnp.logical_or(b == 5, b == 6))
        def _():
            p = 1 - b % 2
            along_z(b, p, 7, p, p).start()

    def step(b, carry):
        pl.when(b < NZ)(lambda: multiply(b))
        pl.when(b < NZ - 1)(lambda: pass_on(b + 1))
        pl.when(jnp.logical_and(b != 1, b <= NZ))(lambda: relay(jnp.maximum(b - 1, 0)))
        pl.when(b >= 3)(lambda: collect(b - 3))
        return carry

    lax.fori_loop(0, NZ + 3, step, 0)

    best = jnp.max(jnp.transpose(col[...].reshape(OWNED, 128)), axis=0, keepdims=True)

    def exchanged(phase, row, combine, meanwhile):
        ex[phase, 0] = row

        def sent(source, target, device):
            return remote(
                ex.at[phase, source], ex.at[phase, target],
                es_sem.at[phase, 1], er_sem.at[phase, 1], device,
            )

        sibling = remote(
            ex.at[phase, 0], ex.at[phase, 1], es_sem.at[phase, 0], er_sem.at[phase, 0], at(dc=1)
        )
        sibling.start()
        for k, (dy, dz) in enumerate(FAR):
            for dc in (0, 1):
                sent(0, 3 + 2 * k + dc, at(dy=dy, dz=dz, dc=dc)).start()
        sibling.wait_recv()
        ex[phase, 2] = combine(row, ex[phase, 1])
        for k, (dy, dz) in enumerate(NEAR):
            sent(2, 3 + 2 * len(FAR) + k, at(dy=dy, dz=dz)).start()
        meanwhile()
        arrived = ex.at[phase, pl.ds(3, LANDED)]
        everyone = remote(
            arrived, arrived, es_sem.at[phase, 1], er_sem.at[phase, 1], at(dz=1)
        )
        sibling.wait_send()
        everyone.wait_recv()
        row = ex[phase, 2]
        for k in range(LANDED):
            row = combine(row, ex[phase, 3 + k])
        return row, everyone

    def settle(b, carry):
        for h in (0, 1):
            pl.when(b >= 1)(along_z(b, h, b, h, h).wait_send)
            to_sibling(b, h).wait_send()
            first_hop(b, h).wait_send()
            second_hop(b, h, 0).wait_send()
            second_hop(b, h, 1).wait_send()
        return carry

    def transposed():
        for k, (dy, dx) in enumerate(PLANE):
            if dy or dx:
                piece(k, dy, dx).wait_send()
            else:
                pl.when(jnp.logical_not(stays))(lambda: piece(k, 0, 0).wait_send())
        lax.fori_loop(0, NZ, settle, 0)
        for g in (0, 1):
            for lo in range(0, COLS, 128):
                n = min(128, COLS - lo)
                tile = acc[4 * g:4 * g + 4, :, lo:lo + n].reshape(128, n)
                lanes = slice(128 * g, 128 * g + 128)
                tile = jnp.transpose(tile)
                logits_t[lo:lo + n, lanes] = tile
                a = jnp.exp(tile - best[:, lanes])
                a4 = (a * a) * (a * a)
                e4[lo:lo + n, lanes] = a4
                e5[lo:lo + n, lanes] = a4 * a

    top, sent_top = exchanged(0, best, jnp.maximum, transposed)

    cut = math.exp(-sharpness * minp_offset)

    scale = jnp.exp(best - top)
    scale4 = (scale * scale) * (scale * scale)
    scale5 = scale4 * scale

    def kept(rows):
        return (e5[rows, :] * scale5) / (e4[rows, :] * scale4 + cut)

    def add_rows(k, total):
        mass = kept(pl.ds(pl.multiple_of(k * STEP, 8), STEP))
        return total + jnp.sum(mass.reshape(STEP // 8, 8, OWNED), axis=0)

    total = lax.fori_loop(0, TAIL // STEP, add_rows, jnp.zeros((8, OWNED), jnp.float32))
    total = jnp.sum(total, axis=0, keepdims=True) + jnp.sum(
        kept(slice(TAIL, COLS)), axis=0, keepdims=True
    )

    def filtered(v):
        shifted = v - top
        u = sharpness * (shifted + minp_offset)
        return shifted + (jnp.minimum(u, 0.0) - jnp.log1p(jnp.exp(-jnp.abs(u))))

    def filter_all():
        def rows(k, carry):
            here = pl.ds(pl.multiple_of(k * STEP, 8), STEP)
            gated[here, :] = filtered(logits_t[here, :])
            return carry

        lax.fori_loop(0, TAIL // STEP, rows, 0)
        gated[TAIL:COLS, :] = filtered(logits_t[TAIL:COLS, :])

    total, sent_total = exchanged(1, total, jnp.add, filter_all)
    lnt_out[...] = jnp.log(total)

    sent_top.wait_send()
    sent_total.wait_send()


def body(states, head):
    dma = pltpu.SemaphoreType.DMA
    f32, bf16 = jnp.float32, jnp.bfloat16
    gated, lnt = pl.pallas_call(
        kernel,
        out_shape=(
            jax.ShapeDtypeStruct((COLS, OWNED), f32),
            jax.ShapeDtypeStruct((1, OWNED), f32),
        ),
        in_specs=[pl.BlockSpec(memory_space=pltpu.HBM)] * 2,
        out_specs=(pl.BlockSpec(memory_space=pltpu.VMEM),) * 2,
        scratch_shapes=[
            pltpu.VMEM((COLS, DEPTH), bf16),
            pltpu.VMEM((DEPTH, COLS), bf16),
            pltpu.VMEM((NY * NX, LOCAL, DEPTH), bf16),
            pltpu.VMEM((NZ, BLOCK, DEPTH), bf16),
            pltpu.VMEM((NZ, BLOCK, COLS), f32),
            pltpu.VMEM((NZ, 2, PIECE, COLS), bf16),
            pltpu.VMEM((NZ, 2, PIECE, COLS), bf16),
            pltpu.VMEM((NZ, 2, 2, PIECE, COLS), bf16),
            pltpu.VMEM((NZ, 2, 2, PIECE, COLS), bf16),
            pltpu.VMEM((NZ, 32, COLS), f32),
            pltpu.VMEM((COLS, OWNED), f32),
            pltpu.VMEM((COLS, OWNED), f32),
            pltpu.VMEM((COLS, OWNED), f32),
            pltpu.VMEM((NZ, 32, 128), f32),
            pltpu.VMEM((2, 3 + LANDED, 1, OWNED), f32),
            dma,
            dma,
            dma((len(PLANE),)), dma((len(PLANE),)),
            dma((NZ, 2)), dma((NZ, 2)),
            dma((NZ, 2)), dma((NZ, 2)),
            dma((NZ, 2)), dma((NZ, 2)),
            dma((NZ, 2, 2)), dma((NZ, 2, 2)),
            dma((2, 2)), dma((2, 2)),
        ],
        compiler_params=pltpu.CompilerParams(
            collective_id=0, has_side_effects=True, vmem_limit_bytes=48 * 1024 * 1024
        ),
        name="minp",
    )(
        pltpu.with_memory_space_constraint(states, pltpu.HBM),
        pltpu.with_memory_space_constraint(head.T, pltpu.HBM),
    )
    return jnp.maximum(gated - lnt, -logp_floor).T


def solution(mesh):
    torus = Mesh(
        mesh.devices.reshape(NY, NZ, NC, NX),
        ("y", "z", "c", "x"),
    )
    return jax.shard_map(
        body,
        mesh=torus,
        in_specs=(P(VOCAB_HIDDEN, None), P("x", VOCAB)),
        out_specs=P("x", VOCAB),
        check_vma=False,
    )
```

```python
import math

import jax
import jax.numpy as jnp
from jax import lax
from jax.experimental import pallas as pl
from jax.experimental.pallas import tpu as pltpu
from jax.sharding import Mesh
from jax.sharding import PartitionSpec as P

MESH = pl.DeviceIdType.MESH
VOCAB = ("y", "z", "c")
VOCAB_HIDDEN = ("y", "z", "c", "x")
NX, NY, NZ, NC = 4, 4, 8, 2

sharpness = 4.0
minp_offset = math.log(10.0)
logp_floor = 30.0

BLOCK = 128
HALF = 64
SHARE = 32
PIECE = 16
LOCAL = 4
OWNED = 256
DEPTH = 1792
COLS = 2020
CHUNKS = ((0, 512), (512, 512), (1024, 512), (1536, 484))
POWER = 7
STEP = 224
TAIL = 9 * STEP
BANDS = ((0, 256), (256, 512), (768, 512), (1280, 740))

PLANE = [(dy, dx) for dy in range(NY) for dx in range(NX)]
PLANE.sort(key=lambda p: -(min(p[0], NY - p[0]) + min(p[1], NX - p[1])))
CHIPS = [(dy, dz) for dy in range(NY) for dz in range(NZ) if dy or dz]
AWAY = {p: min(p[0], NY - p[0]) + min(p[1], NZ - p[1]) for p in CHIPS}
CHIPS.sort(key=lambda p: -AWAY[p])
FAR = [p for p in CHIPS if AWAY[p] >= 5]
NEAR = [p for p in CHIPS if AWAY[p] < 5]
LANDED = 2 * len(FAR) + len(NEAR)


def coded(v):
    v2 = v * v
    v3 = v2 * v
    return (v3 * (v2 * v2)).astype(jnp.bfloat16)


def decoded(w):
    w = w.astype(jnp.float32)
    r = jnp.exp2(jnp.log2(jnp.abs(w)) * (1.0 / POWER))
    return jnp.where(w < 0.0, -r, r)


def lane_max(v):
    n = v.shape[1]
    best = v[:, 0:128]
    for lo in range(128, n, 128):
        part = v[:, lo:min(lo + 128, n)]
        if part.shape[1] < 128:
            fill = jnp.full((v.shape[0], 128 - part.shape[1]), -jnp.inf, v.dtype)
            part = jnp.concatenate([part, fill], axis=1)
        best = jnp.maximum(best, part)
    return best


def kernel(
    states, head, gated, lnt_out,
    staged, raw, weights, xin, st, prod, s1out, s1in, s2out, s2in, acc, logits_t, e4, e5, col, ex,
    s_sem, w_sem, xl_sem, xs_sem, xr_sem, zs_sem, zr_sem, cs_sem, cr_sem,
    s1s_sem, s1r_sem, s2s_sem, s2r_sem, es_sem, er_sem,
):
    x, y, z, c = (lax.axis_index(n) for n in ("x", "y", "z", "c"))

    def at(dy=0, dz=0, dx=0, dc=0):
        return (
            (y + dy) % NY if dy else y,
            (z + dz) % NZ if dz else z,
            1 - c if dc else c,
            (x + dx) % NX if dx else x,
        )

    def remote(src, dst, send, recv, device):
        return pltpu.make_async_remote_copy(
            src_ref=src, dst_ref=dst, send_sem=send, recv_sem=recv,
            device_id=device, device_id_type=MESH,
        )

    s_copy = pltpu.make_async_copy(states, staged, s_sem)
    s_copy.start()
    w_copy = pltpu.make_async_copy(head, raw, w_sem)
    w_copy.start()
    keeper = y // 2
    slot = (y % 2) * 8 + c * NX + x
    stays = keeper == c

    barrier = pltpu.get_barrier_semaphore()

    def greet(device):
        pl.semaphore_signal(barrier, inc=1, device_id=device, device_id_type=MESH)

    for dx in range(NX):
        for j in range(2):
            for cc in range(NC):
                sender = (2 * c + j, z, cc, (x + dx) % NX)
                if dx:
                    greet(sender)
                else:
                    @pl.when(jnp.logical_or(2 * c + j != y, cc != c))
                    def _():
                        greet(sender)
    for device in (at(dz=1), at(dz=NZ - 1), at(dc=1)):
        greet(device)
    s_copy.wait()
    pl.semaphore_wait(barrier, 19 - stays.astype(jnp.int32))

    def piece(k, dy, dx):
        to = (x + dx) % NX
        return remote(
            staged.at[:, pl.ds(pl.multiple_of(to * DEPTH, 128), DEPTH)], xin.at[slot],
            xs_sem.at[k], xr_sem.at[slot], ((y + dy) % NY, z, keeper, to),
        )

    own_piece = pltpu.make_async_copy(
        staged.at[:, pl.ds(pl.multiple_of(x * DEPTH, 128), DEPTH)], xin.at[slot], xl_sem
    )
    for k, (dy, dx) in enumerate(PLANE):
        if dy or dx:
            piece(k, dy, dx).start()
        else:
            pl.when(jnp.logical_not(stays))(lambda: piece(k, 0, 0).start())
            pl.when(stays)(own_piece.start)

    w_copy.wait()
    for lo in range(0, COLS, 256):
        n = min(256, COLS - lo)
        weights[:, lo:lo + n] = jnp.transpose(raw[lo:lo + n, :])

    pl.when(stays)(own_piece.wait)
    for k in range(4 * NX):
        arrived = remote(xin.at[k], xin.at[k], xs_sem.at[k], xr_sem.at[k], at(dc=1))
        pl.when(jnp.logical_or(jnp.logical_not(stays), k != slot))(arrived.wait_recv)
    for j in range(2):
        for cc in range(NC):
            pieces = [xin[j * 8 + cc * NX + k].astype(jnp.float32) for k in range(NX)]
            rows = pl.ds(pl.multiple_of(cc * HALF + c * SHARE + j * PIECE, PIECE), PIECE)
            st[0, rows, :] = jnp.concatenate(pieces, axis=0).astype(jnp.bfloat16)

    def share(b, h):
        return st.at[b, pl.ds(pl.multiple_of(h * HALF + c * SHARE, SHARE), SHARE), :]

    def along_z(source, source_h, target, target_h, way):
        return remote(
            share(source, source_h), share(target, target_h),
            zs_sem.at[target, target_h], zr_sem.at[target, target_h],
            (y, (z + 1 - 2 * way + NZ) % NZ, c, x),
        )

    def to_sibling(b, h):
        return remote(share(b, h), share(b, h), cs_sem.at[b, h], cr_sem.at[b, h], at(dc=1))

    for h in (0, 1):
        to_sibling(0, h).start()
    for way in (0, 1):
        along_z(0, 0, 1, way, way).start()

    right, left, across = (x + 1) % NX, (x + NX - 1) % NX, (x + 2) % NX

    def first_hop(b, h):
        return remote(
            s1out.at[b, h], s1in.at[b, h], s1s_sem.at[b, h], s1r_sem.at[b, h],
            at(dx=1 if h == 0 else NX - 1),
        )

    def second_hop(b, h, part):
        return remote(
            s2out.at[b, h, part], s2in.at[b, h, part], s2s_sem.at[b, h, part], s2r_sem.at[b, h, part],
            at(dx=1 if h == 0 else NX - 1),
        )

    def rows_for(h, d):
        return pl.ds(pl.multiple_of(h * HALF + d * PIECE, PIECE), PIECE)

    def multiply(b):
        for h in (0, 1):
            to_sibling(b, h).wait_recv()
        for lo, n in CHUNKS:
            prod[b, :, lo:lo + n] = jnp.dot(
                st[b], weights[:, lo:lo + n], preferred_element_type=jnp.float32
            )
        for h in (0, 1):
            for lo, n in CHUNKS:
                s1out[b, h, :, lo:lo + n] = coded(prod[b, rows_for(h, across), lo:lo + n])
            first_hop(b, h).start()
        for h in (0, 1):
            to = right if h == 0 else left
            for lo, n in CHUNKS:
                s2out[b, h, 0, :, lo:lo + n] = coded(prod[b, rows_for(1 - h, to), lo:lo + n])
            second_hop(b, h, 0).start()

    def relay(b):
        for h in (0, 1):
            to = right if h == 0 else left
            first_hop(b, h).wait_recv()
            for lo, n in CHUNKS:
                s2out[b, h, 1, :, lo:lo + n] = coded(
                    prod[b, rows_for(h, to), lo:lo + n] + decoded(s1in[b, h, :, lo:lo + n])
                )
            second_hop(b, h, 1).start()

    def collect(b):
        alone = jnp.logical_or(b == 0, b == NZ - 1)
        s = (b + 1) // 2
        for h in (0, 1):
            second_hop(b, 1 - h, 0).wait_recv()
            second_hop(b, h, 1).wait_recv()
            block = jnp.where(alone, z + s, z + NZ + (2 * h - 1) * s) % NZ
            core = jnp.where(alone, h, 1 - b % 2)
            mine = pl.ds(pl.multiple_of(core * PIECE, PIECE), PIECE)
            best = None
            for lo, n in CHUNKS:
                logits = prod[b, rows_for(h, x), lo:lo + n] + (
                    decoded(s2in[b, h, 1, :, lo:lo + n])
                    + decoded(s2in[b, 1 - h, 0, :, lo:lo + n])
                )
                acc[block, mine, lo:lo + n] = logits
                part = lane_max(logits)
                best = part if best is None else jnp.maximum(best, part)
            col[block, mine, :] = best

    def pass_on(b):
        for h in (0, 1):
            along_z(b, h, b, h, h).wait_recv()

            @pl.when(b <= 4)
            def _():
                along_z(b, h, b + 2, h, h).start()

            to_sibling(b, h).start()

        @pl.when(jnp.logical_or(b == 5, b == 6))
        def _():
            p = 1 - b % 2
            along_z(b, p, 7, p, p).start()

    def step(b, carry):
        pl.when(b < NZ)(lambda: multiply(b))

        @pl.when(b == 0)
        def _():
            for way in (0, 1):
                along_z(0, 1, 2, way, way).start()

        pl.when(b < NZ - 1)(lambda: pass_on(b + 1))
        pl.when(jnp.logical_and(b != 1, b <= NZ))(lambda: relay(jnp.maximum(b - 1, 0)))
        pl.when(b >= 3)(lambda: collect(b - 3))
        return carry

    lax.fori_loop(0, NZ + 3, step, 0)

    best = jnp.max(jnp.transpose(col[...].reshape(OWNED, 128)), axis=0, keepdims=True)

    def exchanged(phase, row, combine, meanwhile):
        ex[phase, 0] = row

        def sent(source, target, device):
            return remote(
                ex.at[phase, source], ex.at[phase, target],
                es_sem.at[phase, 1], er_sem.at[phase, 1], device,
            )

        sibling = remote(
            ex.at[phase, 0], ex.at[phase, 1], es_sem.at[phase, 0], er_sem.at[phase, 0], at(dc=1)
        )
        sibling.start()
        for k, (dy, dz) in enumerate(FAR):
            for dc in (0, 1):
                sent(0, 3 + 2 * k + dc, at(dy=dy, dz=dz, dc=dc)).start()
        sibling.wait_recv()
        ex[phase, 2] = combine(row, ex[phase, 1])
        for k, (dy, dz) in enumerate(NEAR):
            sent(2, 3 + 2 * len(FAR) + k, at(dy=dy, dz=dz)).start()
        meanwhile()
        arrived = ex.at[phase, pl.ds(3, LANDED)]
        everyone = remote(
            arrived, arrived, es_sem.at[phase, 1], er_sem.at[phase, 1], at(dz=1)
        )
        sibling.wait_send()
        everyone.wait_recv()
        row = ex[phase, 2]
        for k in range(LANDED):
            row = combine(row, ex[phase, 3 + k])
        return row, everyone

    def settle(b, carry):
        for h in (0, 1):
            pl.when(b >= 1)(along_z(b, h, b, h, h).wait_send)
            to_sibling(b, h).wait_send()
            first_hop(b, h).wait_send()
            second_hop(b, h, 0).wait_send()
            second_hop(b, h, 1).wait_send()
        return carry

    def transposed():
        for k, (dy, dx) in enumerate(PLANE):
            if dy or dx:
                piece(k, dy, dx).wait_send()
            else:
                pl.when(jnp.logical_not(stays))(lambda: piece(k, 0, 0).wait_send())
        lax.fori_loop(0, NZ, settle, 0)
        for g in (0, 1):
            for lo in range(0, COLS, 128):
                n = min(128, COLS - lo)
                tile = acc[4 * g:4 * g + 4, :, lo:lo + n].reshape(128, n)
                lanes = slice(128 * g, 128 * g + 128)
                tile = jnp.transpose(tile)
                logits_t[lo:lo + n, lanes] = tile
                a = jnp.exp(tile - best[:, lanes])
                a4 = (a * a) * (a * a)
                e4[lo:lo + n, lanes] = a4
                e5[lo:lo + n, lanes] = a4 * a

    top, sent_top = exchanged(0, best, jnp.maximum, transposed)

    cut = math.exp(-sharpness * minp_offset)

    scale = jnp.exp(best - top)
    scale4 = (scale * scale) * (scale * scale)
    scale5 = scale4 * scale

    def kept(rows):
        return (e5[rows, :] * scale5) / (e4[rows, :] * scale4 + cut)

    def add_rows(k, total):
        mass = kept(pl.ds(pl.multiple_of(k * STEP, 8), STEP))
        return total + jnp.sum(mass.reshape(STEP // 8, 8, OWNED), axis=0)

    total = lax.fori_loop(0, TAIL // STEP, add_rows, jnp.zeros((8, OWNED), jnp.float32))
    total = jnp.sum(total, axis=0, keepdims=True) + jnp.sum(
        kept(slice(TAIL, COLS)), axis=0, keepdims=True
    )

    def filtered(v):
        shifted = v - top
        u = sharpness * (shifted + minp_offset)
        return shifted + (jnp.minimum(u, 0.0) - jnp.log1p(jnp.exp(-jnp.abs(u))))

    def filter_all():
        def rows(k, carry):
            here = pl.ds(pl.multiple_of(k * STEP, 8), STEP)
            gated[here, :] = filtered(logits_t[here, :])
            return carry

        lax.fori_loop(0, TAIL // STEP, rows, 0)
        gated[TAIL:COLS, :] = filtered(logits_t[TAIL:COLS, :])

    total, sent_total = exchanged(1, total, jnp.add, filter_all)
    lnt_out[...] = jnp.log(total)

    sent_top.wait_send()
    sent_total.wait_send()


def floored(gated, lnt, out, result, sems):
    copies = []
    for k, (lo, n) in enumerate(BANDS):
        result[lo:lo + n, :] = jnp.maximum(gated[lo:lo + n, :] - lnt[...], -logp_floor)
        copies.append(
            pltpu.make_async_copy(result.at[lo:lo + n, :], out.at[lo:lo + n, :], sems.at[k])
        )
        copies[-1].start()
    for copy in copies:
        copy.wait()


def body(states, head):
    dma = pltpu.SemaphoreType.DMA
    f32, bf16 = jnp.float32, jnp.bfloat16
    gated, lnt = pl.pallas_call(
        kernel,
        out_shape=(
            jax.ShapeDtypeStruct((COLS, OWNED), f32),
            jax.ShapeDtypeStruct((1, OWNED), f32),
        ),
        in_specs=[pl.BlockSpec(memory_space=pltpu.HBM)] * 2,
        out_specs=(pl.BlockSpec(memory_space=pltpu.VMEM),) * 2,
        scratch_shapes=[
            pltpu.VMEM((LOCAL, NX * DEPTH), bf16),
            pltpu.VMEM((COLS, DEPTH), bf16),
            pltpu.VMEM((DEPTH, COLS), bf16),
            pltpu.VMEM((NY * NX, LOCAL, DEPTH), bf16),
            pltpu.VMEM((NZ, BLOCK, DEPTH), bf16),
            pltpu.VMEM((NZ, BLOCK, COLS), f32),
            pltpu.VMEM((NZ, 2, PIECE, COLS), bf16),
            pltpu.VMEM((NZ, 2, PIECE, COLS), bf16),
            pltpu.VMEM((NZ, 2, 2, PIECE, COLS), bf16),
            pltpu.VMEM((NZ, 2, 2, PIECE, COLS), bf16),
            pltpu.VMEM((NZ, 32, COLS), f32),
            pltpu.VMEM((COLS, OWNED), f32),
            pltpu.VMEM((COLS, OWNED), f32),
            pltpu.VMEM((COLS, OWNED), f32),
            pltpu.VMEM((NZ, 32, 128), f32),
            pltpu.VMEM((2, 3 + LANDED, 1, OWNED), f32),
            dma,
            dma,
            dma,
            dma((len(PLANE),)), dma((len(PLANE),)),
            dma((NZ, 2)), dma((NZ, 2)),
            dma((NZ, 2)), dma((NZ, 2)),
            dma((NZ, 2)), dma((NZ, 2)),
            dma((NZ, 2, 2)), dma((NZ, 2, 2)),
            dma((2, 2)), dma((2, 2)),
        ],
        compiler_params=pltpu.CompilerParams(
            collective_id=0, has_side_effects=True, vmem_limit_bytes=48 * 1024 * 1024
        ),
        name="minp",
    )(
        pltpu.with_memory_space_constraint(states, pltpu.HBM),
        pltpu.with_memory_space_constraint(head.T, pltpu.HBM),
    )
    return pl.pallas_call(
        floored,
        out_shape=jax.ShapeDtypeStruct((COLS, OWNED), f32),
        in_specs=[pl.BlockSpec(memory_space=pltpu.VMEM)] * 2,
        out_specs=pl.BlockSpec(memory_space=pl.ANY),
        scratch_shapes=[pltpu.VMEM((COLS, OWNED), f32), dma((len(BANDS),))],
        compiler_params=pltpu.CompilerParams(vmem_limit_bytes=8 * 1024 * 1024),
        name="floored",
    )(gated, lnt).T


def solution(mesh):
    torus = Mesh(
        mesh.devices.reshape(NY, NZ, NC, NX),
        ("y", "z", "c", "x"),
    )
    return jax.shard_map(
        body,
        mesh=torus,
        in_specs=(P(VOCAB_HIDDEN, None), P("x", VOCAB)),
        out_specs=P("x", VOCAB),
        check_vma=False,
    )
```

```python
import math

import jax
import jax.numpy as jnp
from jax import lax
from jax.experimental import pallas as pl
from jax.experimental.pallas import tpu as pltpu
from jax.sharding import Mesh
from jax.sharding import PartitionSpec as P

MESH = pl.DeviceIdType.MESH
VOCAB = ("y", "z", "c")
VOCAB_HIDDEN = ("y", "z", "c", "x")
NX, NY, NZ, NC = 4, 4, 8, 2

sharpness = 4.0
minp_offset = math.log(10.0)
logp_floor = 30.0

BLOCK = 128
HALF = 64
SHARE = 32
PIECE = 16
LOCAL = 4
OWNED = 256
DEPTH = 1792
COLS = 2020
CHUNKS = ((0, 512), (512, 512), (1024, 512), (1536, 484))
POWER = 7
STEP = 224
TAIL = 9 * STEP
BANDS = ((0, 256), (256, 512), (768, 512), (1280, 740))

PLANE = [(dy, dx) for dy in range(NY) for dx in range(NX)]
PLANE.sort(key=lambda p: -(min(p[0], NY - p[0]) + min(p[1], NX - p[1])))
CHIPS = [(dy, dz) for dy in range(NY) for dz in range(NZ) if dy or dz]
AWAY = {p: min(p[0], NY - p[0]) + min(p[1], NZ - p[1]) for p in CHIPS}
CHIPS.sort(key=lambda p: -AWAY[p])
FAR = [p for p in CHIPS if AWAY[p] >= 5]
NEAR = [p for p in CHIPS if AWAY[p] < 5]
LANDED = 2 * len(FAR) + len(NEAR)


def coded(v):
    v2 = v * v
    v3 = v2 * v
    return (v3 * (v2 * v2)).astype(jnp.bfloat16)


def decoded(w):
    w = w.astype(jnp.float32)
    r = jnp.exp2(jnp.log2(jnp.abs(w)) * (1.0 / POWER))
    return jnp.where(w < 0.0, -r, r)


def lane_max(v):
    n = v.shape[1]
    best = v[:, 0:128]
    for lo in range(128, n, 128):
        part = v[:, lo:min(lo + 128, n)]
        if part.shape[1] < 128:
            fill = jnp.full((v.shape[0], 128 - part.shape[1]), -jnp.inf, v.dtype)
            part = jnp.concatenate([part, fill], axis=1)
        best = jnp.maximum(best, part)
    return best


def kernel(
    states, head, gated, lnt_out,
    staged, raw, weights, xin, st, prod, s1out, s1in, s2out, s2in, acc, logits_t, e4, e5, col, ex,
    s_sem, w_sem, xl_sem, xs_sem, xr_sem, zs_sem, zr_sem, cs_sem, cr_sem,
    s1s_sem, s1r_sem, s2s_sem, s2r_sem, es_sem, er_sem,
):
    x, y, z, c = (lax.axis_index(n) for n in ("x", "y", "z", "c"))

    def at(dy=0, dz=0, dx=0, dc=0):
        return (
            (y + dy) % NY if dy else y,
            (z + dz) % NZ if dz else z,
            1 - c if dc else c,
            (x + dx) % NX if dx else x,
        )

    def remote(src, dst, send, recv, device):
        return pltpu.make_async_remote_copy(
            src_ref=src, dst_ref=dst, send_sem=send, recv_sem=recv,
            device_id=device, device_id_type=MESH,
        )

    s_copy = pltpu.make_async_copy(states, staged, s_sem)
    s_copy.start()
    w_copy = pltpu.make_async_copy(head, raw, w_sem)
    w_copy.start()
    keeper = y // 2
    slot = (y % 2) * 8 + c * NX + x
    stays = keeper == c

    barrier = pltpu.get_barrier_semaphore()

    def greet(device):
        pl.semaphore_signal(barrier, inc=1, device_id=device, device_id_type=MESH)

    for dx in (2, 1, 3, 0):
        for j in range(2):
            for cc in range(NC):
                sender = (2 * c + j, z, cc, (x + dx) % NX)
                if dx:
                    greet(sender)
                else:
                    @pl.when(jnp.logical_or(2 * c + j != y, cc != c))
                    def _():
                        greet(sender)
    for device in (at(dz=1), at(dz=NZ - 1), at(dc=1)):
        greet(device)
    s_copy.wait()
    pl.semaphore_wait(barrier, 19 - stays.astype(jnp.int32))

    def piece(k, dy, dx):
        to = (x + dx) % NX
        return remote(
            staged.at[:, pl.ds(pl.multiple_of(to * DEPTH, 128), DEPTH)], xin.at[slot],
            xs_sem.at[k], xr_sem.at[slot], ((y + dy) % NY, z, keeper, to),
        )

    own_piece = pltpu.make_async_copy(
        staged.at[:, pl.ds(pl.multiple_of(x * DEPTH, 128), DEPTH)], xin.at[slot], xl_sem
    )
    for k, (dy, dx) in enumerate(PLANE):
        if dy or dx:
            piece(k, dy, dx).start()
        else:
            pl.when(jnp.logical_not(stays))(lambda: piece(k, 0, 0).start())
            pl.when(stays)(own_piece.start)

    w_copy.wait()
    for lo in range(0, COLS, 256):
        n = min(256, COLS - lo)
        weights[:, lo:lo + n] = jnp.transpose(raw[lo:lo + n, :])

    pl.when(stays)(own_piece.wait)
    for k in range(4 * NX):
        arrived = remote(xin.at[k], xin.at[k], xs_sem.at[k], xr_sem.at[k], at(dc=1))
        pl.when(jnp.logical_or(jnp.logical_not(stays), k != slot))(arrived.wait_recv)
    for j in range(2):
        for cc in range(NC):
            pieces = [xin[j * 8 + cc * NX + k].astype(jnp.float32) for k in range(NX)]
            rows = pl.ds(pl.multiple_of(cc * HALF + c * SHARE + j * PIECE, PIECE), PIECE)
            st[0, rows, :] = jnp.concatenate(pieces, axis=0).astype(jnp.bfloat16)

    def share(b, h):
        return st.at[b, pl.ds(pl.multiple_of(h * HALF + c * SHARE, SHARE), SHARE), :]

    def along_z(source, source_h, target, target_h, way):
        return remote(
            share(source, source_h), share(target, target_h),
            zs_sem.at[target, target_h], zr_sem.at[target, target_h],
            (y, (z + 1 - 2 * way + NZ) % NZ, c, x),
        )

    def to_sibling(b, h):
        return remote(share(b, h), share(b, h), cs_sem.at[b, h], cr_sem.at[b, h], at(dc=1))

    for way in (0, 1):
        along_z(0, 0, 1, way, way).start()
    for h in (0, 1):
        to_sibling(0, h).start()

    right, left, across = (x + 1) % NX, (x + NX - 1) % NX, (x + 2) % NX

    def first_hop(b, h):
        return remote(
            s1out.at[b, h], s1in.at[b, h], s1s_sem.at[b, h], s1r_sem.at[b, h],
            at(dx=1 if h == 0 else NX - 1),
        )

    def second_hop(b, h, part):
        return remote(
            s2out.at[b, h, part], s2in.at[b, h, part], s2s_sem.at[b, h, part], s2r_sem.at[b, h, part],
            at(dx=1 if h == 0 else NX - 1),
        )

    def rows_for(h, d):
        return pl.ds(pl.multiple_of(h * HALF + d * PIECE, PIECE), PIECE)

    def multiply(b):
        for h in (0, 1):
            to_sibling(b, h).wait_recv()
        for lo, n in CHUNKS:
            prod[b, :, lo:lo + n] = jnp.dot(
                st[b], weights[:, lo:lo + n], preferred_element_type=jnp.float32
            )
        for h in (0, 1):
            for lo, n in CHUNKS:
                s1out[b, h, :, lo:lo + n] = coded(prod[b, rows_for(h, across), lo:lo + n])
            first_hop(b, h).start()
        for h in (0, 1):
            to = right if h == 0 else left
            for lo, n in CHUNKS:
                s2out[b, h, 0, :, lo:lo + n] = coded(prod[b, rows_for(1 - h, to), lo:lo + n])
            second_hop(b, h, 0).start()

    def relay(b):
        for h in (0, 1):
            to = right if h == 0 else left
            first_hop(b, h).wait_recv()
            for lo, n in CHUNKS:
                s2out[b, h, 1, :, lo:lo + n] = coded(
                    prod[b, rows_for(h, to), lo:lo + n] + decoded(s1in[b, h, :, lo:lo + n])
                )
            second_hop(b, h, 1).start()

    def collect(b):
        alone = jnp.logical_or(b == 0, b == NZ - 1)
        s = (b + 1) // 2
        for h in (0, 1):
            second_hop(b, 1 - h, 0).wait_recv()
            second_hop(b, h, 1).wait_recv()
            block = jnp.where(alone, z + s, z + NZ + (2 * h - 1) * s) % NZ
            core = jnp.where(alone, h, 1 - b % 2)
            mine = pl.ds(pl.multiple_of(core * PIECE, PIECE), PIECE)
            best = None
            for lo, n in CHUNKS:
                logits = prod[b, rows_for(h, x), lo:lo + n] + (
                    decoded(s2in[b, h, 1, :, lo:lo + n])
                    + decoded(s2in[b, 1 - h, 0, :, lo:lo + n])
                )
                acc[block, mine, lo:lo + n] = logits
                part = lane_max(logits)
                best = part if best is None else jnp.maximum(best, part)
            col[block, mine, :] = best

    def pass_on(b):
        for h in (0, 1):
            along_z(b, h, b, h, h).wait_recv()

            @pl.when(b <= 4)
            def _():
                along_z(b, h, b + 2, h, h).start()

            to_sibling(b, h).start()

        @pl.when(jnp.logical_or(b == 5, b == 6))
        def _():
            p = 1 - b % 2
            along_z(b, p, 7, p, p).start()

    def step(b, carry):
        pl.when(b < NZ)(lambda: multiply(b))

        @pl.when(b == 0)
        def _():
            for way in (0, 1):
                along_z(0, 1, 2, way, way).start()

        pl.when(b < NZ - 1)(lambda: pass_on(b + 1))
        pl.when(jnp.logical_and(b != 1, b <= NZ))(lambda: relay(jnp.maximum(b - 1, 0)))
        pl.when(b >= 3)(lambda: collect(b - 3))
        return carry

    lax.fori_loop(0, NZ + 3, step, 0)

    best = jnp.max(jnp.transpose(col[...].reshape(OWNED, 128)), axis=0, keepdims=True)

    def exchanged(phase, row, combine, meanwhile):
        ex[phase, 0] = row

        def sent(source, target, device):
            return remote(
                ex.at[phase, source], ex.at[phase, target],
                es_sem.at[phase, 1], er_sem.at[phase, 1], device,
            )

        sibling = remote(
            ex.at[phase, 0], ex.at[phase, 1], es_sem.at[phase, 0], er_sem.at[phase, 0], at(dc=1)
        )
        sibling.start()
        for k, (dy, dz) in enumerate(FAR):
            for dc in (0, 1):
                sent(0, 3 + 2 * k + dc, at(dy=dy, dz=dz, dc=dc)).start()
        sibling.wait_recv()
        ex[phase, 2] = combine(row, ex[phase, 1])
        for k, (dy, dz) in enumerate(NEAR):
            sent(2, 3 + 2 * len(FAR) + k, at(dy=dy, dz=dz)).start()
        meanwhile()
        arrived = ex.at[phase, pl.ds(3, LANDED)]
        everyone = remote(
            arrived, arrived, es_sem.at[phase, 1], er_sem.at[phase, 1], at(dz=1)
        )
        sibling.wait_send()
        everyone.wait_recv()
        row = ex[phase, 2]
        for k in range(LANDED):
            row = combine(row, ex[phase, 3 + k])
        return row, everyone

    def settle(b, carry):
        for h in (0, 1):
            pl.when(b >= 1)(along_z(b, h, b, h, h).wait_send)
            to_sibling(b, h).wait_send()
            first_hop(b, h).wait_send()
            second_hop(b, h, 0).wait_send()
            second_hop(b, h, 1).wait_send()
        return carry

    def transposed():
        for k, (dy, dx) in enumerate(PLANE):
            if dy or dx:
                piece(k, dy, dx).wait_send()
            else:
                pl.when(jnp.logical_not(stays))(lambda: piece(k, 0, 0).wait_send())
        lax.fori_loop(0, NZ, settle, 0)
        for g in (0, 1):
            for lo in range(0, COLS, 128):
                n = min(128, COLS - lo)
                tile = acc[4 * g:4 * g + 4, :, lo:lo + n].reshape(128, n)
                lanes = slice(128 * g, 128 * g + 128)
                tile = jnp.transpose(tile)
                logits_t[lo:lo + n, lanes] = tile
                a = jnp.exp(tile - best[:, lanes])
                a4 = (a * a) * (a * a)
                e4[lo:lo + n, lanes] = a4
                e5[lo:lo + n, lanes] = a4 * a

    top, sent_top = exchanged(0, best, jnp.maximum, transposed)

    cut = math.exp(-sharpness * minp_offset)

    scale = jnp.exp(best - top)
    scale4 = (scale * scale) * (scale * scale)
    scale5 = scale4 * scale

    def kept(rows):
        return (e5[rows, :] * scale5) / (e4[rows, :] * scale4 + cut)

    def add_rows(k, total):
        mass = kept(pl.ds(pl.multiple_of(k * STEP, 8), STEP))
        return total + jnp.sum(mass.reshape(STEP // 8, 8, OWNED), axis=0)

    total = lax.fori_loop(0, TAIL // STEP, add_rows, jnp.zeros((8, OWNED), jnp.float32))
    total = jnp.sum(total, axis=0, keepdims=True) + jnp.sum(
        kept(slice(TAIL, COLS)), axis=0, keepdims=True
    )

    def filtered(v):
        shifted = v - top
        u = sharpness * (shifted + minp_offset)
        return shifted + (jnp.minimum(u, 0.0) - jnp.log1p(jnp.exp(-jnp.abs(u))))

    def filter_all():
        def rows(k, carry):
            here = pl.ds(pl.multiple_of(k * STEP, 8), STEP)
            gated[here, :] = filtered(logits_t[here, :])
            return carry

        lax.fori_loop(0, TAIL // STEP, rows, 0)
        gated[TAIL:COLS, :] = filtered(logits_t[TAIL:COLS, :])

    total, sent_total = exchanged(1, total, jnp.add, filter_all)
    lnt_out[...] = jnp.log(total)

    sent_top.wait_send()
    sent_total.wait_send()


def floored(gated, lnt, out, result, sems):
    copies = []
    for k, (lo, n) in enumerate(BANDS):
        result[lo:lo + n, :] = jnp.maximum(gated[lo:lo + n, :] - lnt[...], -logp_floor)
        copies.append(
            pltpu.make_async_copy(result.at[lo:lo + n, :], out.at[lo:lo + n, :], sems.at[k])
        )
        copies[-1].start()
    for copy in copies:
        copy.wait()


def body(states, head):
    dma = pltpu.SemaphoreType.DMA
    f32, bf16 = jnp.float32, jnp.bfloat16
    gated, lnt = pl.pallas_call(
        kernel,
        out_shape=(
            jax.ShapeDtypeStruct((COLS, OWNED), f32),
            jax.ShapeDtypeStruct((1, OWNED), f32),
        ),
        in_specs=[pl.BlockSpec(memory_space=pltpu.HBM)] * 2,
        out_specs=(pl.BlockSpec(memory_space=pltpu.VMEM),) * 2,
        scratch_shapes=[
            pltpu.VMEM((LOCAL, NX * DEPTH), bf16),
            pltpu.VMEM((COLS, DEPTH), bf16),
            pltpu.VMEM((DEPTH, COLS), bf16),
            pltpu.VMEM((NY * NX, LOCAL, DEPTH), bf16),
            pltpu.VMEM((NZ, BLOCK, DEPTH), bf16),
            pltpu.VMEM((NZ, BLOCK, COLS), f32),
            pltpu.VMEM((NZ, 2, PIECE, COLS), bf16),
            pltpu.VMEM((NZ, 2, PIECE, COLS), bf16),
            pltpu.VMEM((NZ, 2, 2, PIECE, COLS), bf16),
            pltpu.VMEM((NZ, 2, 2, PIECE, COLS), bf16),
            pltpu.VMEM((NZ, 32, COLS), f32),
            pltpu.VMEM((COLS, OWNED), f32),
            pltpu.VMEM((COLS, OWNED), f32),
            pltpu.VMEM((COLS, OWNED), f32),
            pltpu.VMEM((NZ, 32, 128), f32),
            pltpu.VMEM((2, 3 + LANDED, 1, OWNED), f32),
            dma,
            dma,
            dma,
            dma((len(PLANE),)), dma((len(PLANE),)),
            dma((NZ, 2)), dma((NZ, 2)),
            dma((NZ, 2)), dma((NZ, 2)),
            dma((NZ, 2)), dma((NZ, 2)),
            dma((NZ, 2, 2)), dma((NZ, 2, 2)),
            dma((2, 2)), dma((2, 2)),
        ],
        compiler_params=pltpu.CompilerParams(
            collective_id=0, has_side_effects=True, vmem_limit_bytes=48 * 1024 * 1024
        ),
        name="minp",
    )(
        pltpu.with_memory_space_constraint(states, pltpu.HBM),
        pltpu.with_memory_space_constraint(head.T, pltpu.HBM),
    )
    return pl.pallas_call(
        floored,
        out_shape=jax.ShapeDtypeStruct((COLS, OWNED), f32),
        in_specs=[pl.BlockSpec(memory_space=pltpu.VMEM)] * 2,
        out_specs=pl.BlockSpec(memory_space=pl.ANY),
        scratch_shapes=[pltpu.VMEM((COLS, OWNED), f32), dma((len(BANDS),))],
        compiler_params=pltpu.CompilerParams(vmem_limit_bytes=8 * 1024 * 1024),
        name="floored",
    )(gated, lnt).T


def solution(mesh):
    torus = Mesh(
        mesh.devices.reshape(NY, NZ, NC, NX),
        ("y", "z", "c", "x"),
    )
    return jax.shard_map(
        body,
        mesh=torus,
        in_specs=(P(VOCAB_HIDDEN, None), P("x", VOCAB)),
        out_specs=P("x", VOCAB),
        check_vma=False,
    )
```

```python
import math

import jax
import jax.numpy as jnp
from jax import lax
from jax.experimental import pallas as pl
from jax.experimental.pallas import tpu as pltpu
from jax.sharding import Mesh
from jax.sharding import PartitionSpec as P

MESH = pl.DeviceIdType.MESH
VOCAB = ("y", "z", "c")
VOCAB_HIDDEN = ("y", "z", "c", "x")
NX, NY, NZ, NC = 4, 4, 8, 2

sharpness = 4.0
minp_offset = math.log(10.0)
logp_floor = 30.0

BLOCK = 128
HALF = 64
SHARE = 32
PIECE = 16
LOCAL = 4
OWNED = 256
DEPTH = 1792
COLS = 2020
CHUNKS = ((0, 512), (512, 512), (1024, 512), (1536, 484))
POWER = 7
STEP = 224
TAIL = 9 * STEP
BANDS = ((0, 256), (256, 512), (768, 512), (1280, 740))

PLANE = [(dy, dx) for dy in range(NY) for dx in range(NX)]
PLANE.sort(key=lambda p: -(min(p[0], NY - p[0]) + min(p[1], NX - p[1])))
CHIPS = [(dy, dz) for dy in range(NY) for dz in range(NZ) if dy or dz]
AWAY = {p: min(p[0], NY - p[0]) + min(p[1], NZ - p[1]) for p in CHIPS}
CHIPS.sort(key=lambda p: -AWAY[p])
FAR = [p for p in CHIPS if AWAY[p] >= 4]
NEAR = [p for p in CHIPS if AWAY[p] < 4]
LANDED = 2 * len(FAR) + len(NEAR)


def coded(v):
    v2 = v * v
    v3 = v2 * v
    return (v3 * (v2 * v2)).astype(jnp.bfloat16)


def decoded(w):
    w = w.astype(jnp.float32)
    r = jnp.exp2(jnp.log2(jnp.abs(w)) * (1.0 / POWER))
    return jnp.where(w < 0.0, -r, r)


def lane_max(v):
    n = v.shape[1]
    best = v[:, 0:128]
    for lo in range(128, n, 128):
        part = v[:, lo:min(lo + 128, n)]
        if part.shape[1] < 128:
            fill = jnp.full((v.shape[0], 128 - part.shape[1]), -jnp.inf, v.dtype)
            part = jnp.concatenate([part, fill], axis=1)
        best = jnp.maximum(best, part)
    return best


def kernel(
    states, head, gated, lnt_out,
    staged, raw, weights, xin, st, prod, s1out, s1in, s2out, s2in, acc, logits_t, e4, e5, col, ex,
    s_sem, w_sem, xl_sem, xs_sem, xr_sem, zs_sem, zr_sem, cs_sem, cr_sem,
    s1s_sem, s1r_sem, s2s_sem, s2r_sem, es_sem, er_sem,
):
    x, y, z, c = (lax.axis_index(n) for n in ("x", "y", "z", "c"))

    def at(dy=0, dz=0, dx=0, dc=0):
        return (
            (y + dy) % NY if dy else y,
            (z + dz) % NZ if dz else z,
            1 - c if dc else c,
            (x + dx) % NX if dx else x,
        )

    def remote(src, dst, send, recv, device):
        return pltpu.make_async_remote_copy(
            src_ref=src, dst_ref=dst, send_sem=send, recv_sem=recv,
            device_id=device, device_id_type=MESH,
        )

    s_copy = pltpu.make_async_copy(states, staged, s_sem)
    s_copy.start()
    w_copy = pltpu.make_async_copy(head, raw, w_sem)
    w_copy.start()
    keeper = y // 2
    slot = (y % 2) * 8 + c * NX + x
    stays = keeper == c

    barrier = pltpu.get_barrier_semaphore()

    def greet(device):
        pl.semaphore_signal(barrier, inc=1, device_id=device, device_id_type=MESH)

    for dx in (2, 1, 3, 0):
        for j in range(2):
            for cc in range(NC):
                sender = (2 * c + j, z, cc, (x + dx) % NX)
                if dx:
                    greet(sender)
                else:
                    @pl.when(jnp.logical_or(2 * c + j != y, cc != c))
                    def _():
                        greet(sender)
    for device in (at(dz=1), at(dz=NZ - 1), at(dc=1)):
        greet(device)
    s_copy.wait()
    pl.semaphore_wait(barrier, 19 - stays.astype(jnp.int32))

    def piece(k, dy, dx):
        to = (x + dx) % NX
        return remote(
            staged.at[:, pl.ds(pl.multiple_of(to * DEPTH, 128), DEPTH)], xin.at[slot],
            xs_sem.at[k], xr_sem.at[slot], ((y + dy) % NY, z, keeper, to),
        )

    own_piece = pltpu.make_async_copy(
        staged.at[:, pl.ds(pl.multiple_of(x * DEPTH, 128), DEPTH)], xin.at[slot], xl_sem
    )
    for k, (dy, dx) in enumerate(PLANE):
        if dy or dx:
            piece(k, dy, dx).start()
        else:
            pl.when(jnp.logical_not(stays))(lambda: piece(k, 0, 0).start())
            pl.when(stays)(own_piece.start)

    w_copy.wait()
    for lo in range(0, COLS, 256):
        n = min(256, COLS - lo)
        weights[:, lo:lo + n] = jnp.transpose(raw[lo:lo + n, :])

    pl.when(stays)(own_piece.wait)
    for k in range(4 * NX):
        arrived = remote(xin.at[k], xin.at[k], xs_sem.at[k], xr_sem.at[k], at(dc=1))
        pl.when(jnp.logical_or(jnp.logical_not(stays), k != slot))(arrived.wait_recv)
    for j in range(2):
        for cc in range(NC):
            pieces = [xin[j * 8 + cc * NX + k].astype(jnp.float32) for k in range(NX)]
            rows = pl.ds(pl.multiple_of(cc * HALF + c * SHARE + j * PIECE, PIECE), PIECE)
            st[0, rows, :] = jnp.concatenate(pieces, axis=0).astype(jnp.bfloat16)

    def share(b, h):
        return st.at[b, pl.ds(pl.multiple_of(h * HALF + c * SHARE, SHARE), SHARE), :]

    def along_z(source, source_h, target, target_h, way):
        return remote(
            share(source, source_h), share(target, target_h),
            zs_sem.at[target, target_h], zr_sem.at[target, target_h],
            (y, (z + 1 - 2 * way + NZ) % NZ, c, x),
        )

    def to_sibling(b, h):
        return remote(share(b, h), share(b, h), cs_sem.at[b, h], cr_sem.at[b, h], at(dc=1))

    for way in (0, 1):
        along_z(0, 0, 1, way, way).start()
    for h in (0, 1):
        to_sibling(0, h).start()

    right, left, across = (x + 1) % NX, (x + NX - 1) % NX, (x + 2) % NX

    def first_hop(b, h):
        return remote(
            s1out.at[b, h], s1in.at[b, h], s1s_sem.at[b, h], s1r_sem.at[b, h],
            at(dx=1 if h == 0 else NX - 1),
        )

    def second_hop(b, h, part):
        return remote(
            s2out.at[b, h, part], s2in.at[b, h, part], s2s_sem.at[b, h, part], s2r_sem.at[b, h, part],
            at(dx=1 if h == 0 else NX - 1),
        )

    def rows_for(h, d):
        return pl.ds(pl.multiple_of(h * HALF + d * PIECE, PIECE), PIECE)

    def multiply(b):
        for h in (0, 1):
            to_sibling(b, h).wait_recv()
        for lo, n in CHUNKS:
            prod[b, :, lo:lo + n] = jnp.dot(
                st[b], weights[:, lo:lo + n], preferred_element_type=jnp.float32
            )
        for h in (0, 1):
            for lo, n in CHUNKS:
                s1out[b, h, :, lo:lo + n] = coded(prod[b, rows_for(h, across), lo:lo + n])
            first_hop(b, h).start()
        for h in (0, 1):
            to = right if h == 0 else left
            for lo, n in CHUNKS:
                s2out[b, h, 0, :, lo:lo + n] = coded(prod[b, rows_for(1 - h, to), lo:lo + n])
            second_hop(b, h, 0).start()

    def relay(b):
        for h in (0, 1):
            to = right if h == 0 else left
            first_hop(b, h).wait_recv()
            for lo, n in CHUNKS:
                s2out[b, h, 1, :, lo:lo + n] = coded(
                    prod[b, rows_for(h, to), lo:lo + n] + decoded(s1in[b, h, :, lo:lo + n])
                )
            second_hop(b, h, 1).start()

    def collect(b):
        alone = jnp.logical_or(b == 0, b == NZ - 1)
        s = (b + 1) // 2
        for h in (0, 1):
            second_hop(b, 1 - h, 0).wait_recv()
            second_hop(b, h, 1).wait_recv()
            block = jnp.where(alone, z + s, z + NZ + (2 * h - 1) * s) % NZ
            core = jnp.where(alone, h, 1 - b % 2)
            mine = pl.ds(pl.multiple_of(core * PIECE, PIECE), PIECE)
            best = None
            for lo, n in CHUNKS:
                logits = prod[b, rows_for(h, x), lo:lo + n] + (
                    decoded(s2in[b, h, 1, :, lo:lo + n])
                    + decoded(s2in[b, 1 - h, 0, :, lo:lo + n])
                )
                acc[block, mine, lo:lo + n] = logits
                part = lane_max(logits)
                best = part if best is None else jnp.maximum(best, part)
            col[block, mine, :] = best

    def pass_on(b):
        for h in (0, 1):
            along_z(b, h, b, h, h).wait_recv()

            @pl.when(b <= 4)
            def _():
                along_z(b, h, b + 2, h, h).start()

            to_sibling(b, h).start()

        @pl.when(jnp.logical_or(b == 5, b == 6))
        def _():
            p = 1 - b % 2
            along_z(b, p, 7, p, p).start()

    def step(b, carry):
        pl.when(b < NZ)(lambda: multiply(b))

        @pl.when(b == 0)
        def _():
            for way in (0, 1):
                along_z(0, 1, 2, way, way).start()

        pl.when(b < NZ - 1)(lambda: pass_on(b + 1))
        pl.when(jnp.logical_and(b != 1, b <= NZ))(lambda: relay(jnp.maximum(b - 1, 0)))
        pl.when(b >= 3)(lambda: collect(b - 3))
        return carry

    lax.fori_loop(0, NZ + 3, step, 0)

    best = jnp.max(jnp.transpose(col[...].reshape(OWNED, 128)), axis=0, keepdims=True)

    def exchanged(phase, row, combine, meanwhile):
        ex[phase, 0] = row

        def sent(source, target, device):
            return remote(
                ex.at[phase, source], ex.at[phase, target],
                es_sem.at[phase, 1], er_sem.at[phase, 1], device,
            )

        sibling = remote(
            ex.at[phase, 0], ex.at[phase, 1], es_sem.at[phase, 0], er_sem.at[phase, 0], at(dc=1)
        )
        sibling.start()
        for k, (dy, dz) in enumerate(FAR):
            for dc in (0, 1):
                sent(0, 3 + 2 * k + dc, at(dy=dy, dz=dz, dc=dc)).start()
        sibling.wait_recv()
        ex[phase, 2] = combine(row, ex[phase, 1])
        for k, (dy, dz) in enumerate(NEAR):
            sent(2, 3 + 2 * len(FAR) + k, at(dy=dy, dz=dz)).start()
        meanwhile()
        arrived = ex.at[phase, pl.ds(3, LANDED)]
        everyone = remote(
            arrived, arrived, es_sem.at[phase, 1], er_sem.at[phase, 1], at(dz=1)
        )
        sibling.wait_send()
        everyone.wait_recv()
        row = ex[phase, 2]
        for k in range(LANDED):
            row = combine(row, ex[phase, 3 + k])
        return row, everyone

    def settle(b, carry):
        for h in (0, 1):
            pl.when(b >= 1)(along_z(b, h, b, h, h).wait_send)
            to_sibling(b, h).wait_send()
            first_hop(b, h).wait_send()
            second_hop(b, h, 0).wait_send()
            second_hop(b, h, 1).wait_send()
        return carry

    def transposed():
        for k, (dy, dx) in enumerate(PLANE):
            if dy or dx:
                piece(k, dy, dx).wait_send()
            else:
                pl.when(jnp.logical_not(stays))(lambda: piece(k, 0, 0).wait_send())
        lax.fori_loop(0, NZ, settle, 0)
        for g in (0, 1):
            for lo in range(0, COLS, 128):
                n = min(128, COLS - lo)
                tile = acc[4 * g:4 * g + 4, :, lo:lo + n].reshape(128, n)
                lanes = slice(128 * g, 128 * g + 128)
                tile = jnp.transpose(tile)
                logits_t[lo:lo + n, lanes] = tile
                a = jnp.exp(tile - best[:, lanes])
                a4 = (a * a) * (a * a)
                e4[lo:lo + n, lanes] = a4
                e5[lo:lo + n, lanes] = a4 * a

    top, sent_top = exchanged(0, best, jnp.maximum, transposed)

    cut = math.exp(-sharpness * minp_offset)

    scale = jnp.exp(best - top)
    scale4 = (scale * scale) * (scale * scale)
    scale5 = scale4 * scale

    def kept(rows):
        return e5[rows, :] / (e4[rows, :] * scale4 + cut)

    def add_rows(k, total):
        mass = kept(pl.ds(pl.multiple_of(k * STEP, 8), STEP))
        return total + jnp.sum(mass.reshape(STEP // 8, 8, OWNED), axis=0)

    total = lax.fori_loop(0, TAIL // STEP, add_rows, jnp.zeros((8, OWNED), jnp.float32))
    total = jnp.sum(total, axis=0, keepdims=True) + jnp.sum(
        kept(slice(TAIL, COLS)), axis=0, keepdims=True
    )
    total = total * scale5

    def filtered(v):
        shifted = v - top
        u = sharpness * (shifted + minp_offset)
        return shifted + (jnp.minimum(u, 0.0) - jnp.log1p(jnp.exp(-jnp.abs(u))))

    def filter_all():
        def rows(k, carry):
            here = pl.ds(pl.multiple_of(k * STEP, 8), STEP)
            gated[here, :] = filtered(logits_t[here, :])
            return carry

        lax.fori_loop(0, TAIL // STEP, rows, 0)
        gated[TAIL:COLS, :] = filtered(logits_t[TAIL:COLS, :])

    total, sent_total = exchanged(1, total, jnp.add, filter_all)
    lnt_out[...] = jnp.log(total)

    sent_top.wait_send()
    sent_total.wait_send()


def floored(gated, lnt, out, result, sems):
    copies = []
    for k, (lo, n) in enumerate(BANDS):
        result[lo:lo + n, :] = jnp.maximum(gated[lo:lo + n, :] - lnt[...], -logp_floor)
        copies.append(
            pltpu.make_async_copy(result.at[lo:lo + n, :], out.at[lo:lo + n, :], sems.at[k])
        )
        copies[-1].start()
    for copy in copies:
        copy.wait()


def body(states, head):
    dma = pltpu.SemaphoreType.DMA
    f32, bf16 = jnp.float32, jnp.bfloat16
    gated, lnt = pl.pallas_call(
        kernel,
        out_shape=(
            jax.ShapeDtypeStruct((COLS, OWNED), f32),
            jax.ShapeDtypeStruct((1, OWNED), f32),
        ),
        in_specs=[pl.BlockSpec(memory_space=pltpu.HBM)] * 2,
        out_specs=(pl.BlockSpec(memory_space=pltpu.VMEM),) * 2,
        scratch_shapes=[
            pltpu.VMEM((LOCAL, NX * DEPTH), bf16),
            pltpu.VMEM((COLS, DEPTH), bf16),
            pltpu.VMEM((DEPTH, COLS), bf16),
            pltpu.VMEM((NY * NX, LOCAL, DEPTH), bf16),
            pltpu.VMEM((NZ, BLOCK, DEPTH), bf16),
            pltpu.VMEM((NZ, BLOCK, COLS), f32),
            pltpu.VMEM((NZ, 2, PIECE, COLS), bf16),
            pltpu.VMEM((NZ, 2, PIECE, COLS), bf16),
            pltpu.VMEM((NZ, 2, 2, PIECE, COLS), bf16),
            pltpu.VMEM((NZ, 2, 2, PIECE, COLS), bf16),
            pltpu.VMEM((NZ, 32, COLS), f32),
            pltpu.VMEM((COLS, OWNED), f32),
            pltpu.VMEM((COLS, OWNED), f32),
            pltpu.VMEM((COLS, OWNED), f32),
            pltpu.VMEM((NZ, 32, 128), f32),
            pltpu.VMEM((2, 3 + LANDED, 1, OWNED), f32),
            dma,
            dma,
            dma,
            dma((len(PLANE),)), dma((len(PLANE),)),
            dma((NZ, 2)), dma((NZ, 2)),
            dma((NZ, 2)), dma((NZ, 2)),
            dma((NZ, 2)), dma((NZ, 2)),
            dma((NZ, 2, 2)), dma((NZ, 2, 2)),
            dma((2, 2)), dma((2, 2)),
        ],
        compiler_params=pltpu.CompilerParams(
            collective_id=0, has_side_effects=True, vmem_limit_bytes=48 * 1024 * 1024
        ),
        name="minp",
    )(
        pltpu.with_memory_space_constraint(states, pltpu.HBM),
        pltpu.with_memory_space_constraint(head.T, pltpu.HBM),
    )
    return pl.pallas_call(
        floored,
        out_shape=jax.ShapeDtypeStruct((COLS, OWNED), f32),
        in_specs=[pl.BlockSpec(memory_space=pltpu.VMEM)] * 2,
        out_specs=pl.BlockSpec(memory_space=pl.ANY),
        scratch_shapes=[pltpu.VMEM((COLS, OWNED), f32), dma((len(BANDS),))],
        compiler_params=pltpu.CompilerParams(vmem_limit_bytes=8 * 1024 * 1024),
        name="floored",
    )(gated, lnt).T


def solution(mesh):
    torus = Mesh(
        mesh.devices.reshape(NY, NZ, NC, NX),
        ("y", "z", "c", "x"),
    )
    return jax.shard_map(
        body,
        mesh=torus,
        in_specs=(P(VOCAB_HIDDEN, None), P("x", VOCAB)),
        out_specs=P("x", VOCAB),
        check_vma=False,
    )
```
